512 devices in a mesh: tm: 32 (over z, x), lm: 16 (over y, core).
Axes of the slice: x: 4, y: 8, z: 8, core: 2. Of those that a mesh axis runs over, the one named last changes fastest.
Arguments:
- camera_poses: float32 [6, 32768], P(None, 'tm'), may hold values from -1.5 to 1.5
- landmarks: float32 [3, 262144], P(None, ('tm', 'lm')), may hold values from -5 to 5
- odometry: float32 [6, 32768], P(None, 'tm'), may hold values from -1.5 to 1.5
- odometry_info: float32 [32768], P('tm'), may hold values from 100 to 3000
- observations: bfloat16 [49152, 3, 64, 64], P(('tm', 'lm')), may hold values from -6 to 6
- tile_frame: int32 [49152], P(('tm', 'lm')), may hold values from 0 to 15, as said below
- tile_block: int32 [49152], P(('tm', 'lm')), may hold values from 0 to 127, as said below
- tile_count: int32 [512], P(('tm', 'lm')), may hold values from 38 to 96, as said below
- block_slot: int32 [32, 128], P('tm'), may hold values from 0 to 127, each once within a row
Outputs:
- refined_poses: float32 [6, 32768], P(None, 'tm')
- refined_points: float32 [3, 262144], P(None, ('tm', 'lm'))
The draws below stay inside these ranges and needn't reach their ends.
Inputs may be any that keep to these rules, and one draw needn't show every extreme that they name: `tile_frame`: frame blocks of the slot's own time shard. `tile_block`: landmark block ids of the slot's own time shard. `tile_count`: slots from this count on hold no live tile; some device is full. `block_slot`: each row is a permutation of the 128 block ids.
All inputs are finite; a program needn't handle non-finite values.
Results may differ from the reference program's by a relative error of at most 0.0003.
Values sent between devices are 32-bit elements; how exact they have to be, the bound alone decides.
No kernel may reach another device: no remote copies, remote signals or barrier semaphores. Data moves between devices by JAX's collectives and lax.ppermute only.
A program may use at most 64 MiB of HBM per device.

```python
import math
import jax
import jax.numpy as jnp
from jax import lax

TILE = 64
FRM_DEV = 1024
TILE_CAP = 96
ITERS = 2
FBLK_DEV = 16
FRAMES = 32768
LB_ROW = 128
LANDMARKS = 262144
TILES = 49152
N_TM = 32
N_LM = 16
DEVICES = 512


def tile_lists(key):
    base_key = jax.random.fold_in(key, 17)
    first_key, second_key = jax.random.split(base_key)
    frame_ids = jax.random.randint(first_key, (TILES,), 0, FBLK_DEV)
    spread = max(LB_ROW // FBLK_DEV, 1)
    further = jax.random.randint(second_key, (TILES,), 0, 2 * spread)
    block_ids = (frame_ids * LB_ROW // FBLK_DEV + further) % LB_ROW
    return (frame_ids.astype(jnp.int32), block_ids.astype(jnp.int32))


def draw_tile_frame(key, part):
    return tile_lists(key)[0]


def draw_tile_block(key, part):
    return tile_lists(key)[1]


def draw_tile_count(key, part):
    base_key = jax.random.fold_in(key, 29)
    first_key, second_key = jax.random.split(base_key)
    counts = jax.random.randint(first_key, (DEVICES,), TILE_CAP * 2 // 5, TILE_CAP + 1)
    busiest = jax.random.randint(second_key, (), 0, DEVICES)
    return jnp.where(jnp.arange(DEVICES) == busiest, TILE_CAP, counts).astype(jnp.int32)


def levels(rng, extent, cuts, least, high):
    def one(position, blocks):
        draws = jax.random.uniform(jax.random.fold_in(jax.random.fold_in(rng, 6), position), (blocks,), jnp.float32, least / len(cuts), high / len(cuts))
        return jnp.repeat(jnp.exp(draws), extent[position] // blocks).reshape((-1,) + (1,) * (len(extent) - position - 1))

    level = one(*cuts[0])
    for cut in cuts[1:]:
        level = level * one(*cut)
    return level


def bell_draw(key, dims, deviation, bound, cuts=(), kind=jnp.bfloat16):
    gain = levels(key, dims, cuts, -0.22, 0.18) if cuts else 1.0
    entries = jax.random.normal(key, dims, jnp.float32) * deviation * gain
    return jnp.minimum(jnp.maximum(entries, -bound), bound).astype(kind)


def setup_inputs(seed: int = 0) -> dict:
    splits = jax.random.split(jax.random.key(seed), 10)
    camera_poses = bell_draw(splits[0], (6, FRAMES), 0.3, 1.5, ((1, 32),), jnp.float32)
    landmarks = bell_draw(splits[1], (3, LANDMARKS), 1.0, 5.0, ((1, 512),), jnp.float32)
    odometry = bell_draw(splits[2], (6, FRAMES), 0.3, 1.5, ((1, 32),), jnp.float32)
    odometry_info = jnp.clip(jnp.exp(math.log(3000.0) - 3.4011974 * jax.random.uniform(splits[3], (FRAMES,), jnp.float32) ** levels(splits[3], (FRAMES,), ((0, 32),), -0.2, 0.2)), 100.0, 3000.0)
    observations = bell_draw(splits[4], (TILES, 3, TILE, TILE), 1.0, 6.0, ((0, 512),))
    tile_frame = draw_tile_frame(jax.random.fold_in(splits[9], 71), 0)
    tile_block = draw_tile_block(jax.random.fold_in(splits[9], 71), 0)
    tile_count = draw_tile_count(jax.random.fold_in(splits[9], 71), 0)
    block_slot = jax.vmap(lambda own: jax.random.permutation(own, LB_ROW))(jax.random.split(splits[8], N_TM)).reshape((N_TM, LB_ROW)).astype(jnp.int32)
    return dict(camera_poses=camera_poses, landmarks=landmarks, odometry=odometry, odometry_info=odometry_info, observations=observations, tile_frame=tile_frame, tile_block=tile_block, tile_count=tile_count, block_slot=block_slot)


robust_scale = 4.0
damping = 1.0
moment_pairs = ((0, 0), (1, 1), (2, 2), (0, 1), (0, 2), (1, 2))

def cross_product(left, right):
    return [left[1] * right[2] - left[2] * right[1], left[2] * right[0] - left[0] * right[2], left[0] * right[1] - left[1] * right[0]]

def tile_terms(rotation, offset, points, measured_tiles, live_mask):
    rotation_rows = [rotation[k][:, :, None] for k in range(3)]
    offset_rows = [offset[k][:, :, None] for k in range(3)]
    point_columns = [points[k][:, None, :] for k in range(3)]
    measured = measured_tiles.astype(jnp.float32)
    turned = cross_product(rotation_rows, point_columns)
    residual = [point_columns[k] + turned[k] + offset_rows[k] - measured[:, k] for k in range(3)]
    squared = residual[0] * residual[0] + residual[1] * residual[1] + residual[2] * residual[2]
    weight = live_mask[:, None, None] / (1.0 + squared / robust_scale)
    weighted = [weight * residual[k] for k in range(3)]
    lever = cross_product(point_columns, weighted)
    frame_terms = [lax.optimization_barrier(jnp.sum(lever[k], axis=2)) for k in range(3)]
    frame_terms += [lax.optimization_barrier(jnp.sum(weighted[k], axis=2)) for k in range(3)]
    frame_terms += [lax.optimization_barrier(jnp.sum(weight, axis=2))]
    frame_terms += [lax.optimization_barrier(jnp.sum(weight * point_columns[k], axis=2)) for k in range(3)]
    frame_terms += [lax.optimization_barrier(jnp.sum(weight * (point_columns[a] * point_columns[b]), axis=2)) for a, b in moment_pairs]
    spun = cross_product(rotation_rows, weighted)
    point_terms = [lax.optimization_barrier(jnp.sum(weighted[k] - spun[k], axis=1)) for k in range(3)]
    rotation_square = rotation_rows[0] * rotation_rows[0] + rotation_rows[1] * rotation_rows[1] + rotation_rows[2] * rotation_rows[2]
    point_terms += [lax.optimization_barrier(jnp.sum(weight * (1.0 + rotation_square), axis=1))]
    point_terms += [lax.optimization_barrier(jnp.sum(weight * (rotation_rows[a] * rotation_rows[b]), axis=1)) for a, b in moment_pairs]
    return (jnp.stack(frame_terms, axis=1), jnp.stack(point_terms, axis=1))

def block_solve(matrix, vector):
    dimension = len(vector)
    factor = [[None] * dimension for i in range(dimension)]
    inverse_diag = [None] * dimension
    for i in range(dimension):
        for j in range(i + 1):
            running = matrix[i][j]
            for k in range(j):
                running = running - factor[i][k] * factor[j][k]
            if i == j:
                factor[i][i] = jnp.sqrt(running)
                inverse_diag[i] = 1.0 / factor[i][i]
            else:
                factor[i][j] = running * inverse_diag[j]
    forward = [None] * dimension
    for i in range(dimension):
        running = vector[i]
        for k in range(i):
            running = running - factor[i][k] * forward[k]
        forward[i] = running * inverse_diag[i]
    solution = [None] * dimension
    for i in reversed(range(dimension)):
        running = forward[i]
        for k in range(i + 1, dimension):
            running = running - factor[k][i] * solution[k]
        solution[i] = running * inverse_diag[i]
    return solution

def pose_step(sums, current, link_grad, link_diag):
    moments = [sums[10 + m] for m in range(6)]
    centroid = [sums[7 + m] for m in range(3)]
    counted = sums[6]
    diagonal_add = link_diag + damping
    zero_entry = jnp.zeros_like(counted)
    rotation_block = [[moments[1] + moments[2] + diagonal_add, -moments[3], -moments[4]], [-moments[3], moments[0] + moments[2] + diagonal_add, -moments[5]], [-moments[4], -moments[5], moments[0] + moments[1] + diagonal_add]]
    cross_block = [[zero_entry, -centroid[2], centroid[1]], [centroid[2], zero_entry, -centroid[0]], [-centroid[1], centroid[0], zero_entry]]
    matrix = []
    for i in range(3):
        matrix.append(rotation_block[i] + cross_block[i])
    for i in range(3):
        offset_row = [counted + diagonal_add if i == k else zero_entry for k in range(3)]
        matrix.append([cross_block[k][i] for k in range(3)] + offset_row)
    gradient = [sums[k] + link_grad[k] for k in range(6)]
    solution = block_solve(matrix, gradient)
    return current - jnp.stack(solution)

def point_step(sums, current):
    diagonal = sums[3] + damping
    outer = [sums[4 + m] for m in range(6)]
    matrix = [[diagonal - outer[0], -outer[3], -outer[4]], [-outer[3], diagonal - outer[1], -outer[5]], [-outer[4], -outer[5], diagonal - outer[2]]]
    solution = block_solve(matrix, [sums[0], sums[1], sums[2]])
    return current - jnp.stack(solution)

def reference(camera_poses, landmarks, odometry, odometry_info, observations, tile_frame, tile_block, tile_count, block_slot):
    device_tiles = observations.reshape(DEVICES, TILE_CAP, 3, TILE, TILE)
    device_frames = tile_frame.reshape(DEVICES, TILE_CAP)
    device_blocks = tile_block.reshape(DEVICES, TILE_CAP)
    time_rows = (jnp.arange(DEVICES) // N_LM).astype(jnp.int32)
    poses = camera_poses
    points = landmarks
    for iteration in range(ITERS):

        def device_terms(carry, inputs):
            frame_total, point_total = carry
            tiles_here, frames_here, blocks_here, count_here, time_row = inputs
            frame_start = (time_row * FRM_DEV).astype(jnp.int32)
            point_start = (time_row * (LB_ROW * TILE)).astype(jnp.int32)
            pose_shard = lax.dynamic_slice_in_dim(poses, frame_start, FRM_DEV, 1).reshape(6, FBLK_DEV, TILE)
            picked = jnp.take(pose_shard, frames_here, axis=1)
            window = lax.dynamic_slice_in_dim(points, point_start, LB_ROW * TILE, 1).reshape(3, LB_ROW, TILE)
            slot_table = lax.dynamic_index_in_dim(block_slot, time_row, 0, keepdims=False)
            positions = jnp.take(slot_table, blocks_here).astype(jnp.int32)
            seen_points = jnp.take(window, positions, axis=1)
            live_mask = (jnp.arange(TILE_CAP) < count_here).astype(jnp.float32)
            frame_part, point_part = tile_terms(picked[0:3], picked[3:6], seen_points, tiles_here, live_mask)
            frame_onehot = (frames_here[:, None] == jnp.arange(FBLK_DEV)[None, :]).astype(jnp.float32)
            point_onehot = (positions[:, None] == jnp.arange(LB_ROW)[None, :]).astype(jnp.float32)
            frame_sum = jnp.einsum('tf,tqi->qfi', frame_onehot, frame_part, precision=lax.Precision.HIGHEST).reshape(16, FRM_DEV)
            point_sum = jnp.einsum('tp,tqi->qpi', point_onehot, point_part, precision=lax.Precision.HIGHEST).reshape(10, LB_ROW * TILE)
            frame_total = lax.dynamic_update_slice_in_dim(frame_total, lax.dynamic_slice_in_dim(frame_total, frame_start, FRM_DEV, 1) + frame_sum, frame_start, 1)
            point_total = lax.dynamic_update_slice_in_dim(point_total, lax.dynamic_slice_in_dim(point_total, point_start, LB_ROW * TILE, 1) + point_sum, point_start, 1)
            return ((frame_total, point_total), None)
        starting = (jnp.zeros((16, FRAMES), jnp.float32), jnp.zeros((10, LANDMARKS), jnp.float32))
        totals = lax.scan(device_terms, starting, (device_tiles, device_frames, device_blocks, tile_count, time_rows))[0]
        link_gap = poses[:, 1:] - poses[:, :-1] - odometry[:, :-1]
        link_weight = odometry_info[:-1]
        weighted_gap = link_weight[None, :] * link_gap
        zero_column = jnp.zeros((6, 1), jnp.float32)
        link_grad = jnp.concatenate([-weighted_gap, zero_column], axis=1) + jnp.concatenate([zero_column, weighted_gap], axis=1)
        zero_single = jnp.zeros((1,), jnp.float32)
        link_diag = jnp.concatenate([link_weight, zero_single]) + jnp.concatenate([zero_single, link_weight])
        next_poses = pose_step(totals[0], poses, link_grad, link_diag)
        points = point_step(totals[1], points)
        poses = next_poses
    return (poses, points)
```

```python
import jax
import jax.numpy as jnp
from jax import lax
from jax.experimental import pallas as pl
from jax.experimental.pallas import tpu as pltpu
from jax.sharding import PartitionSpec as P

TILE = 64
ITERS = 2
damping = 1.0
scale = 4.0


def vmem():
    return pl.BlockSpec(memory_space=pltpu.VMEM)


def lanes(shape):
    return lax.broadcasted_iota(jnp.int32, shape, 1)


def half_turn(x):
    return pltpu.roll(x, 64, 1)


def own_block(ref, block):
    pair = jnp.zeros((8, 128), jnp.float32)
    for h in range(8):
        pair = jnp.where(block // 2 == h, ref[:, h * 128 : (h + 1) * 128], pair)
    return jnp.where(block % 2 == 1, half_turn(pair), pair)


def pack_kernel(points_ref, poses_ref, odometry_ref, info_ref, copies_ref, edge_ref, link_ref, rows, chunk):
    owner = lax.axis_index("lm")
    lane = lanes((8, 128))
    rows[...] = jnp.zeros((8, 1024), jnp.float32)
    rows[0:6, :] = odometry_ref[...]
    rows[6:7, :] = info_ref[...]
    current = own_block(rows, owner)
    before = own_block(rows, owner - 1)
    link_ref[:, 0:128] = current
    link_ref[:, 128:256] = jnp.where(lane == 0, pltpu.roll(before, 65, 1), pltpu.roll(current, 1, 1))
    rows[...] = jnp.zeros((8, 1024), jnp.float32)
    rows[0:6, :] = poses_ref[...]
    pose = own_block(rows, owner)
    edge_ref[:, 0:128] = pose
    edge_ref[:, 128:256] = current
    for k in range(3):
        for b in range(8):
            chunk[b : b + 1, k * 64 : (k + 1) * 64] = points_ref[k : k + 1, b * 64 : (b + 1) * 64]
    chunk[:, 192:256] = half_turn(pose)[:, 64:128]
    whole = chunk[...]
    for d in range(copies_ref.shape[0]):
        copies_ref[d] = whole


def split(x, parts):
    pieces = []
    for _ in range(parts - 1):
        pieces.append(x.astype(jnp.bfloat16))
        x = x - pieces[-1].astype(jnp.float32)
    pieces.append(x.astype(jnp.bfloat16))
    return pieces


def dot(a, b):
    return lax.dot_general(a, b, (((1,), (0,)), ((), ())), preferred_element_type=jnp.float32)


def dot_t(a, b):
    return lax.dot_general(a, b, (((1,), (1,)), ((), ())), preferred_element_type=jnp.float32)


def tiles_kernel(count_ref, window_ref, seen_ref, frame_ref, block_ref, slot_ref, out_ref, pose, point, fsum, psum):
    slots = frame_ref.shape[1]
    row = lax.broadcasted_iota(jnp.int32, (128, slots), 0)
    frame = frame_ref[...]
    named = jnp.where(block_ref[...] == row, 1.0, 0.0).astype(jnp.bfloat16)
    table = jnp.broadcast_to(slot_ref[...].astype(jnp.float32), (8, 128)).astype(jnp.bfloat16)
    position = dot(table, named)[0:1].astype(jnp.int32)
    held = position == row
    live = lanes((1, slots)) < count_ref[0]
    pick = jnp.where(held, 1.0, 0.0).astype(jnp.bfloat16)
    turned = jnp.transpose(window_ref[...].reshape(128, 256), (1, 0))
    pieces = split(turned, 3)
    point[...] = sum(dot(piece[0:192], pick) for piece in pieces)
    for k in range(6):
        pick = jnp.where(frame * 8 + k == row, 1.0, 0.0).astype(jnp.bfloat16)
        pose[k * 64 : (k + 1) * 64, :] = sum(dot(piece[192:256], pick) for piece in pieces)
    psum[...] = jnp.zeros_like(psum)

    def step(i, carry):
        w = [jnp.broadcast_to(pose[pl.ds(k * 64 + i, 1), :], (8, slots)) for k in range(3)]
        t = [jnp.broadcast_to(pose[pl.ds(192 + k * 64 + i, 1), :], (8, slots)) for k in range(3)]
        w00, w11, w22 = w[0] * w[0], w[1] * w[1], w[2] * w[2]
        m00, m11, m22 = 1.0 + (w11 + w22), 1.0 + (w00 + w22), 1.0 + (w00 + w11)
        m01, m02, m12 = w[0] * w[1], w[0] * w[2], w[1] * w[2]
        total = [None] * 16
        for g in range(4):
            seen = [seen_ref[k, i, g * 16 : (g + 1) * 16, :].astype(jnp.float32) for k in range(3)]
            for h in range(2):
                at = g * 16 + h * 8
                x = [point[k * 64 + at : k * 64 + at + 8, :] for k in range(3)]
                o = [seen[k][h * 8 : (h + 1) * 8] for k in range(3)]
                r0 = (x[0] + t[0] - o[0]) + (w[1] * x[2] - w[2] * x[1])
                r1 = (x[1] + t[1] - o[1]) + (w[2] * x[0] - w[0] * x[2])
                r2 = (x[2] + t[2] - o[2]) + (w[0] * x[1] - w[1] * x[0])
                c = 1.0 / (scale + (r0 * r0 + r1 * r1 + r2 * r2))
                c0, c1, c2 = c * r0, c * r1, c * r2
                y = [c * x[k] for k in range(3)]
                terms = [
                    x[1] * c2 - x[2] * c1,
                    x[2] * c0 - x[0] * c2,
                    x[0] * c1 - x[1] * c0,
                    c0,
                    c1,
                    c2,
                    c,
                    y[0],
                    y[1],
                    y[2],
                    y[0] * x[0],
                    y[1] * x[1],
                    y[2] * x[2],
                    y[0] * x[1],
                    y[0] * x[2],
                    y[1] * x[2],
                ]
                total = terms if total[0] is None else [p + q for p, q in zip(total, terms)]
                terms = [
                    c * m00,
                    c * m11,
                    c * m22,
                    c * m01,
                    c * m02,
                    c * m12,
                    c0 - (w[1] * c2 - w[2] * c1),
                    c1 - (w[2] * c0 - w[0] * c2),
                    c2 - (w[0] * c1 - w[1] * c0),
                ]
                for q, term in enumerate(terms):
                    psum[q * 64 + at : q * 64 + at + 8, :] += term
        for q in range(16):
            fsum[pl.ds(q * 64 + i, 1), :] = jnp.sum(total[q], axis=0, keepdims=True)
        return carry

    lax.fori_loop(0, 64, step, 0)
    weight = jnp.where(live, scale, 0.0)
    own = jnp.where(frame == lax.broadcasted_iota(jnp.int32, (16, slots), 0), weight, 0.0).astype(jnp.bfloat16)
    frames = sum(dot_t(own, piece) for piece in split(fsum[...], 3))
    for r in range(8):
        out_ref[:, 40 + r, :] = frames[:, r * 128 : (r + 1) * 128]
    own = jnp.where(held, weight, 0.0).astype(jnp.bfloat16)
    for q in range(5):
        wide = 128 if q < 4 else 64
        part = sum(dot_t(own, piece) for piece in split(psum[q * 128 : q * 128 + wide, :], 3))
        if wide < 128:
            part = jnp.concatenate([part, jnp.zeros_like(part)], axis=1)
        out_ref[:, q * 8 : (q + 1) * 8, :] = part.reshape(16, 8, 128)


def solve3(m00, m11, m22, m01, m02, m12, b0, b1, b2):
    i0 = 1.0 / m00
    l1, l2 = m01 * i0, m02 * i0
    d1 = m11 - l1 * m01
    e = m12 - l1 * m02
    i1 = 1.0 / d1
    l3 = e * i1
    d2 = m22 - l2 * m02 - l3 * e
    y1 = b1 - l1 * b0
    y2 = b2 - l2 * b0 - l3 * y1
    x2 = y2 / d2
    x1 = y1 * i1 - l3 * x2
    x0 = b0 * i0 - l1 * x1 - l2 * x2
    return x0, x1, x2


def new_poses(sums, window_ref, link_ref, edge_ref, first_edge_ref, scratch):
    owner, shard = lax.axis_index("lm"), lax.axis_index("tm")
    owners, shards = lax.axis_size("lm"), lax.axis_size("tm")
    lane = lanes((8, 128))
    current = half_turn(window_ref[owner, :, 128:256])
    before = half_turn(window_ref[jnp.maximum(owner - 1, 0), :, 128:256])
    after = half_turn(window_ref[jnp.minimum(owner + 1, owners - 1), :, 128:256])
    outside = edge_ref[:, 0:128]
    initial, final = owner == 0, owner == owners - 1
    before = jnp.where(initial, outside, before)
    after = jnp.where(final, outside, after)
    previous = jnp.where(lane == 0, pltpu.roll(before, 65, 1), pltpu.roll(current, 1, 1))
    following = jnp.where(lane == 63, pltpu.roll(after, 63, 1), pltpu.roll(current, 127, 1))
    motion = link_ref[:, 0:128]
    motion_before = link_ref[:, 128:256]
    outside = pltpu.roll(first_edge_ref[:, 128:256], 65, 1)
    motion_before = jnp.where((lane == 0) & initial, outside, motion_before)
    ends = (lane[0:1] == 63) & final & (shard == shards - 1)
    starts = (lane[0:1] == 0) & initial & (shard == 0)
    weight_after = jnp.where(ends, 0.0, motion[6:7])
    weight_before = jnp.where(starts, 0.0, motion_before[6:7])
    scratch[0:8] = weight_before * (current - previous - motion_before) - weight_after * (
        following - current - motion
    )
    scratch[8:16] = sums
    scratch[16:24] = half_turn(sums)
    f = [scratch[8 + 8 * (q % 2) + q // 2 : 9 + 8 * (q % 2) + q // 2, :] for q in range(16)]
    g = [f[k] + scratch[k : k + 1, :] for k in range(6)]
    diagonal = weight_after + weight_before + damping
    s, c, m = f[6] + diagonal, f[7:10], f[10:16]
    inverse = 1.0 / s
    d = [c[k] * inverse for k in range(3)]
    n00 = m[1] + m[2] + diagonal - (c[1] * d[1] + c[2] * d[2])
    n11 = m[0] + m[2] + diagonal - (c[0] * d[0] + c[2] * d[2])
    n22 = m[0] + m[1] + diagonal - (c[0] * d[0] + c[1] * d[1])
    n01, n02, n12 = c[0] * d[1] - m[3], c[0] * d[2] - m[4], c[1] * d[2] - m[5]
    b0 = g[0] - (d[1] * g[5] - d[2] * g[4])
    b1 = g[1] - (d[2] * g[3] - d[0] * g[5])
    b2 = g[2] - (d[0] * g[4] - d[1] * g[3])
    x0, x1, x2 = solve3(n00, n11, n22, n01, n02, n12, b0, b1, b2)
    x3 = (g[3] + (c[1] * x2 - c[2] * x1)) * inverse
    x4 = (g[4] + (c[2] * x0 - c[0] * x2)) * inverse
    x5 = (g[5] + (c[0] * x1 - c[1] * x0)) * inverse
    for k, x in enumerate((x0, x1, x2, x3, x4, x5)):
        scratch[k : k + 1, :] = x
    return current - scratch[0:8]


def new_points(sums_ref, window_ref):
    owner = lax.axis_index("lm")
    owned = window_ref[owner]
    x = [owned[:, 0:128], half_turn(owned[:, 0:128]), owned[:, 128:256]]
    q = []
    for k in range(5):
        pair = sums_ref[0, k * 8 : (k + 1) * 8, :]
        for d in range(1, sums_ref.shape[0]):
            pair = pair + sums_ref[d, k * 8 : (k + 1) * 8, :]
        q += [pair, half_turn(pair)]
    moved = solve3(q[0] + damping, q[1] + damping, q[2] + damping, -q[3], -q[4], -q[5], q[6], q[7], q[8])
    return [x[k] - moved[k] for k in range(3)]


def frame_sums(sums_ref):
    total = sums_ref[0, 40:48, :]
    for d in range(1, sums_ref.shape[0]):
        total = total + sums_ref[d, 40:48, :]
    return total


def update_kernel(sums_ref, window_ref, link_ref, edge_ref, copies_ref, sent_ref, scratch):
    lower = lanes((8, 128)) < 64
    pose = new_poses(frame_sums(sums_ref), window_ref, link_ref, edge_ref, edge_ref, scratch)
    sent_ref[...] = pose
    x = new_points(sums_ref, window_ref)
    left = jnp.where(lower, x[0], half_turn(x[1]))
    right = jnp.where(lower, x[2], half_turn(pose))
    for d in range(copies_ref.shape[0]):
        copies_ref[d, :, 0:128] = left
        copies_ref[d, :, 128:256] = right


def last_poses_kernel(sums_ref, window_ref, link_ref, edge_ref, first_edge_ref, copies_ref, scratch):
    pose = new_poses(frame_sums(sums_ref), window_ref, link_ref, edge_ref, first_edge_ref, scratch)
    for d in range(copies_ref.shape[0]):
        copies_ref[d] = pose


def last_points_kernel(sums_ref, window_ref, out_ref):
    x = new_points(sums_ref, window_ref)
    for k in range(3):
        for b in range(8):
            out_ref[k : k + 1, b * 64 : (b + 1) * 64] = x[k][b : b + 1, 0:64]


def spread_kernel(poses_ref, out_ref):
    lower = lanes((8, 128)) < 64
    for h in range(8):
        pair = jnp.where(lower, poses_ref[2 * h], half_turn(poses_ref[2 * h + 1]))
        out_ref[:, h * 128 : (h + 1) * 128] = pair[0:6]


def call(kernel, outs, scratch, *args, smem=0):
    specs = [pl.BlockSpec(memory_space=pltpu.SMEM)] * smem + [vmem()] * (len(args) - smem)
    single = not isinstance(outs, (list, tuple))
    return pl.pallas_call(
        kernel,
        out_shape=outs,
        in_specs=specs,
        out_specs=vmem() if single else [vmem()] * len(outs),
        scratch_shapes=scratch,
        compiler_params=pltpu.CompilerParams(vmem_limit_bytes=24 << 20),
    )(*args)


def exchange(array):
    return lax.all_to_all(array, "lm", 0, 0, tiled=True)


def on_device(
    camera_poses,
    landmarks,
    odometry,
    odometry_info,
    observations,
    tile_frame,
    tile_block,
    tile_count,
    block_slot,
):
    owners, shards = lax.axis_size("lm"), lax.axis_size("tm")
    slots = observations.shape[0]
    f32 = jnp.float32
    seen = jnp.transpose(observations, (1, 2, 3, 0))
    to_edges = []
    for a in range(shards - 1):
        to_edges.append((a * owners + owners - 1, (a + 1) * owners))
        to_edges.append(((a + 1) * owners, a * owners + owners - 1))

    def edges(array):
        return lax.ppermute(array, ("tm", "lm"), to_edges)

    chunks = jax.ShapeDtypeStruct((owners, 8, 256), f32)
    wide = jax.ShapeDtypeStruct((8, 256), f32)
    narrow = jax.ShapeDtypeStruct((8, 128), f32)
    small = [pltpu.VMEM((24, 128), f32)]
    copies, sent, link = call(
        pack_kernel,
        [chunks, wide, wide],
        [pltpu.VMEM((8, 1024), f32), pltpu.VMEM((8, 256), f32)],
        landmarks,
        camera_poses,
        odometry,
        odometry_info[None, :],
    )
    first_edge = None
    for iteration in range(ITERS):
        window = exchange(copies)
        edge = edges(sent)
        sums = call(
            tiles_kernel,
            jax.ShapeDtypeStruct((owners, 48, 128), f32),
            [
                pltpu.VMEM((384, slots), f32),
                pltpu.VMEM((192, slots), f32),
                pltpu.VMEM((1024, slots), f32),
                pltpu.VMEM((576, slots), f32),
            ],
            tile_count,
            window,
            seen,
            tile_frame[None, :],
            tile_block[None, :],
            block_slot,
            smem=1,
        )
        sums = exchange(sums)
        if iteration == 0:
            first_edge = edge
            copies, sent = call(update_kernel, [chunks, narrow], small, sums, window, link, edge)
    copies = call(
        last_poses_kernel,
        jax.ShapeDtypeStruct((owners, 8, 128), f32),
        small,
        sums,
        window,
        link,
        edge,
        first_edge,
    )
    gathered = exchange(copies)
    points = call(last_points_kernel, jax.ShapeDtypeStruct(landmarks.shape, f32), [], sums, window)
    poses = call(spread_kernel, jax.ShapeDtypeStruct(camera_poses.shape, f32), [], gathered)
    return (poses, points)


def solution(mesh):
    return jax.shard_map(
        on_device,
        mesh=mesh,
        in_specs=(
            P(None, "tm"),
            P(None, ("tm", "lm")),
            P(None, "tm"),
            P("tm"),
            P(("tm", "lm"), None, None, None),
            P(("tm", "lm")),
            P(("tm", "lm")),
            P(("tm", "lm")),
            P("tm", None),
        ),
        out_specs=(P(None, "tm"), P(None, ("tm", "lm"))),
        check_vma=False,
    )
```

```python
import functools

import jax
import jax.numpy as jnp
from jax import lax
from jax.experimental import pallas as pl
from jax.experimental.pallas import tpu as pltpu
from jax.sharding import PartitionSpec as P

TILE = 64
ITERS = 2
SLOTS = 96
EXTRA = 128 - SLOTS
GROUPS = SLOTS // EXTRA
PLAIN = TILE * SLOTS // 128
FOLDED = TILE - PLAIN
damping = 1.0
scale = 4.0


def lanes(shape):
    return lax.broadcasted_iota(jnp.int32, shape, 1)


def half_turn(x):
    return pltpu.roll(x, 64, 1)


def own_block(ref, block):
    pair = jnp.zeros((8, 128), jnp.float32)
    for h in range(8):
        pair = jnp.where(block // 2 == h, ref[:, h * 128 : (h + 1) * 128], pair)
    return jnp.where(block % 2 == 1, half_turn(pair), pair)


def pack_kernel(
    count_ref,
    points_hbm,
    poses_hbm,
    odometry_hbm,
    info_hbm,
    frame_hbm,
    block_hbm,
    slot_hbm,
    copies_hbm,
    edge_hbm,
    link_hbm,
    names_hbm,
    more_names_hbm,
    points,
    poses,
    odometry,
    info,
    frame,
    block,
    slot,
    rows,
    chunk,
    edge,
    link_ref,
    names_ref,
    sems,
):
    loads = [
        pltpu.make_async_copy(source, target, sems.at[n])
        for n, (source, target) in enumerate(
            [
                (poses_hbm, poses),
                (points_hbm, points),
                (odometry_hbm, odometry),
                (info_hbm, info),
                (frame_hbm, frame),
                (block_hbm, block),
                (slot_hbm, slot),
            ]
        )
    ]
    for load in loads:
        load.start()
    rows[...] = jnp.zeros((8, 1024), jnp.float32)
    owner = lax.axis_index("lm")
    lane = lanes((8, 128))
    for load in loads:
        load.wait()
    rows[0:6, :] = poses[...]
    pose = own_block(rows, owner)
    for k in range(3):
        for b in range(8):
            chunk[b : b + 1, k * 64 : (k + 1) * 64] = points[k : k + 1, b * 64 : (b + 1) * 64]
    chunk[:, 192:256] = half_turn(pose)[:, 64:128]
    owners = copies_hbm.shape[0]
    sends = [pltpu.make_async_copy(chunk, copies_hbm.at[d], sems.at[10 + d]) for d in range(owners)]
    for send in sends:
        send.start()
    rows[0:6, :] = odometry[...]
    rows[6:7, :] = info[...]
    current = own_block(rows, owner)
    before = own_block(rows, owner - 1)
    edge[:, 0:128] = pose
    edge[:, 128:256] = current
    sends.append(pltpu.make_async_copy(edge, edge_hbm, sems.at[7]))
    sends[-1].start()
    link_ref[:, 0:128] = current
    link_ref[:, 128:256] = jnp.where(lane == 0, pltpu.roll(before, 65, 1), pltpu.roll(current, 1, 1))
    sends.append(pltpu.make_async_copy(link_ref, link_hbm, sems.at[8]))
    sends[-1].start()
    slots = frame.shape[1]
    row = lax.broadcasted_iota(jnp.int32, (128, slots), 0)
    named = jnp.where(block[...] == row, 1.0, 0.0).astype(jnp.bfloat16)
    table = jnp.broadcast_to(slot[...].astype(jnp.float32), (8, 128)).astype(jnp.bfloat16)
    position = dot(table, named)[0:1].astype(jnp.int32)
    live = lanes((1, slots)) < count_ref[0]
    names_ref[...] = jnp.full(names_ref.shape, -1, jnp.int32)
    names_ref[0:1, 0:slots] = jnp.where(live, frame[...], -1)
    names_ref[1:2, 0:slots] = jnp.where(live, position, -1)
    for n in range(2):
        name = names_ref[...][n : n + 1]
        for g in range(GROUPS):
            folded = jnp.where(lane[0:1] < SLOTS, name, pltpu.roll(name, SLOTS - g * EXTRA, 1))
            names_ref[2 + n * GROUPS + g : 3 + n * GROUPS + g, :] = folded
    sends.append(pltpu.make_async_copy(names_ref, names_hbm, sems.at[9]))
    sends[-1].start()
    sends.append(pltpu.make_async_copy(names_ref, more_names_hbm, sems.at[10 + owners]))
    sends[-1].start()
    for send in sends:
        send.wait()


def split(x, parts):
    pieces = []
    for _ in range(parts - 1):
        pieces.append(x.astype(jnp.bfloat16))
        x = x - pieces[-1].astype(jnp.float32)
    pieces.append(x.astype(jnp.bfloat16))
    return pieces


def dot(a, b):
    return lax.dot_general(a, b, (((1,), (0,)), ((), ())), preferred_element_type=jnp.float32)


def dot_t(a, b):
    return lax.dot_general(a, b, (((1,), (1,)), ((), ())), preferred_element_type=jnp.float32)


def fold_kernel(seen_hbm, out_hbm, seen, folded, sems):
    parts = [pl.ds(PLAIN, FOLDED)] + [pl.ds(g * FOLDED, FOLDED) for g in range(GROUPS)]
    loads = [
        pltpu.make_async_copy(seen_hbm.at[:, part], seen.at[:, part], sems.at[n]) for n, part in enumerate(parts)
    ]
    for load in loads:
        load.start()
    loads[0].wait()
    stores = []
    for g in range(GROUPS):
        loads[1 + g].wait()

        def step(m, carry):
            for k in range(3):
                for r in range(0, TILE, 16):
                    wide = seen[k, g * FOLDED + m, r : r + 16, :]
                    more = seen[k, PLAIN + m, r : r + 16, g * EXTRA : (g + 1) * EXTRA]
                    folded[k, g * FOLDED + m, r : r + 16, :] = jnp.concatenate([wide, more], axis=1)
            return carry

        lax.fori_loop(0, FOLDED, step, 0)
        part = parts[1 + g]
        stores.append(pltpu.make_async_copy(folded.at[:, part], out_hbm.at[:, part], sems.at[1 + GROUPS + g]))
        stores[-1].start()
    for store in stores:
        store.wait()


def tiles_kernel(window_ref, names_ref, seen_hbm, out_hbm, near_hbm, *scratch):
    near_ref, seen_ref, pose, point, fsum, psum, sums, sems, load_sems = scratch
    owner, owners = lax.axis_index("lm"), lax.axis_size("lm")
    chunks = load_sems.shape[0]
    pieces = PLAIN // chunks

    def load(n):
        part = pl.ds(n * pieces, pieces)
        return pltpu.make_async_copy(seen_hbm.at[:, part], seen_ref.at[:, part], load_sems.at[n])

    ahead = 2
    for n in range(ahead):
        load(n).start()
    near_ref[0] = window_ref[owner]
    near_ref[1] = window_ref[jnp.maximum(owner - 1, 0)]
    near_ref[2] = window_ref[jnp.minimum(owner + 1, owners - 1)]
    turned = split(jnp.transpose(window_ref[...].reshape(128, 256), (1, 0)), 3)
    put_near = pltpu.make_async_copy(near_ref, near_hbm, sems.at[7])
    put_near.start()
    row = lax.broadcasted_iota(jnp.int32, (128, 128), 0)
    lane = lanes((FOLDED, 128))
    points = jnp.concatenate([piece[0:192] for piece in turned], axis=0)
    for g in range(GROUPS):
        frame, position = names_ref[2 + g : 3 + g, :], names_ref[2 + GROUPS + g : 3 + GROUPS + g, :]
        pick = jnp.where(position == row, 1.0, 0.0).astype(jnp.bfloat16)
        found = dot(points, pick)
        point[g * 192 : (g + 1) * 192, :] = found[0:192] + (found[192:384] + found[384:576])
        at = 192 + g * FOLDED
        poses = jnp.concatenate(
            [piece[r : r + FOLDED] for r in (at, 192 + PLAIN) for piece in turned], axis=0
        )
        for k in range(6):
            pick = jnp.where(frame * 8 + k == row, 1.0, 0.0).astype(jnp.bfloat16)
            found = [dot(poses, pick)[n * FOLDED : (n + 1) * FOLDED] for n in range(6)]
            found = [found[n] + (found[n + 1] + found[n + 2]) for n in (0, 3)]
            pose[k * PLAIN + g * FOLDED : k * PLAIN + (g + 1) * FOLDED, :] = jnp.where(lane < SLOTS, *found)
    psum[...] = jnp.zeros_like(psum)

    def step(g, i, carry):
        w = [jnp.broadcast_to(pose[pl.ds(k * PLAIN + i, 1), :], (8, 128)) for k in range(3)]
        t = [jnp.broadcast_to(pose[pl.ds((3 + k) * PLAIN + i, 1), :], (8, 128)) for k in range(3)]
        w00, w11, w22 = w[0] * w[0], w[1] * w[1], w[2] * w[2]
        m00, m11, m22 = 1.0 + (w11 + w22), 1.0 + (w00 + w22), 1.0 + (w00 + w11)
        m01, m02, m12 = w[0] * w[1], w[0] * w[2], w[1] * w[2]
        total = [None] * 16
        for part in range(0, TILE, 16):
            seen = [seen_ref[k, i, part : part + 16, :].astype(jnp.float32) for k in range(3)]
            for h in range(2):
                at = part + h * 8
                x = [point[(g * 3 + k) * 64 + at : (g * 3 + k) * 64 + at + 8, :] for k in range(3)]
                o = [seen[k][h * 8 : (h + 1) * 8] for k in range(3)]
                r0 = (x[0] + t[0] - o[0]) + (w[1] * x[2] - w[2] * x[1])
                r1 = (x[1] + t[1] - o[1]) + (w[2] * x[0] - w[0] * x[2])
                r2 = (x[2] + t[2] - o[2]) + (w[0] * x[1] - w[1] * x[0])
                c = 1.0 / (scale + (r0 * r0 + r1 * r1 + r2 * r2))
                c0, c1, c2 = c * r0, c * r1, c * r2
                y = [c * x[k] for k in range(3)]
                terms = [
                    x[1] * c2 - x[2] * c1,
                    x[2] * c0 - x[0] * c2,
                    x[0] * c1 - x[1] * c0,
                    c0,
                    c1,
                    c2,
                    c,
                    y[0],
                    y[1],
                    y[2],
                    y[0] * x[0],
                    y[1] * x[1],
                    y[2] * x[2],
                    y[0] * x[1],
                    y[0] * x[2],
                    y[1] * x[2],
                ]
                total = terms if total[0] is None else [p + q for p, q in zip(total, terms)]
                terms = [
                    c * m00,
                    c * m11,
                    c * m22,
                    c * m01,
                    c * m02,
                    c * m12,
                    c0 - (w[1] * c2 - w[2] * c1),
                    c1 - (w[2] * c0 - w[0] * c2),
                    c2 - (w[0] * c1 - w[1] * c0),
                ]
                for q, term in enumerate(terms):
                    psum[q * 64 + at : q * 64 + at + 8, :] += term
        for q in range(16):
            fsum[pl.ds(q * 64 + i, 1), :] = jnp.sum(total[q], axis=0, keepdims=True)
        return carry

    def chunk(g, n, carry):
        load(n).wait()

        @pl.when(n + ahead < chunks)
        def _():
            load(n + ahead).start()

        return lax.fori_loop(n * pieces, (n + 1) * pieces, functools.partial(step, g), carry)

    lane = lanes((64, 128))
    each = chunks // GROUPS
    for g in range(GROUPS):
        lax.fori_loop(g * each, (g + 1) * each, functools.partial(chunk, g), 0)
        mine = (lane >= g * EXTRA) & (lane < (g + 1) * EXTRA)
        for q in range(9):
            part = psum[q * 64 : (q + 1) * 64, :]
            back = jnp.where(mine, pltpu.roll(part, (g + 1) * EXTRA, 1), 0.0)
            psum[q * 64 : (q + 1) * 64, :] = jnp.where(lane < SLOTS, part, 0.0) + back
    lane = lanes((FOLDED, 128))
    for q in range(16):
        back = jnp.zeros((FOLDED, 128), jnp.float32)
        for g in range(GROUPS):
            part = fsum[q * 64 + g * FOLDED : q * 64 + (g + 1) * FOLDED, :]
            back = jnp.where((lane >= g * EXTRA) & (lane < (g + 1) * EXTRA), pltpu.roll(part, (g + 1) * EXTRA, 1), back)
        fsum[q * 64 + PLAIN : (q + 1) * 64, :] = back
    frame, position = names_ref[0:1, :], names_ref[1:2, :]
    held = position == row
    own = jnp.where(frame == lax.broadcasted_iota(jnp.int32, (16, 128), 0), scale, 0.0).astype(jnp.bfloat16)
    frames = sum(dot_t(own, piece) for piece in split(fsum[...], 3))
    for r in range(8):
        sums[:, 40 + r, :] = frames[:, r * 128 : (r + 1) * 128]
    put_near.wait()
    stores = [pltpu.make_async_copy(sums.at[:, 40:48], out_hbm.at[:, 40:48], sems.at[5])]
    stores[0].start()
    own = jnp.where(held, scale, 0.0).astype(jnp.bfloat16)
    for q in range(5):
        wide = 128 if q < 4 else 64
        part = sum(dot_t(own, piece) for piece in split(psum[q * 128 : q * 128 + wide, :], 3))
        if wide < 128:
            part = jnp.concatenate([part, jnp.zeros_like(part)], axis=1)
        rows = slice(q * 8, (q + 1) * 8)
        sums[:, rows, :] = part.reshape(16, 8, 128)
        stores.append(pltpu.make_async_copy(sums.at[:, rows], out_hbm.at[:, rows], sems.at[q]))
        stores[-1].start()
    for store in stores:
        store.wait()


def solve3(m00, m11, m22, m01, m02, m12, b0, b1, b2):
    i0 = 1.0 / m00
    l1, l2 = m01 * i0, m02 * i0
    d1 = m11 - l1 * m01
    e = m12 - l1 * m02
    i1 = 1.0 / d1
    l3 = e * i1
    d2 = m22 - l2 * m02 - l3 * e
    y1 = b1 - l1 * b0
    y2 = b2 - l2 * b0 - l3 * y1
    x2 = y2 / d2
    x1 = y1 * i1 - l3 * x2
    x0 = b0 * i0 - l1 * x1 - l2 * x2
    return x0, x1, x2


def new_poses(sums, near_ref, link_ref, edge_ref, first_edge_ref, scratch):
    owner, shard = lax.axis_index("lm"), lax.axis_index("tm")
    owners, shards = lax.axis_size("lm"), lax.axis_size("tm")
    lane = lanes((8, 128))
    current, before, after = (half_turn(near_ref[n, :, 128:256]) for n in range(3))
    outside = edge_ref[:, 0:128]
    initial, final = owner == 0, owner == owners - 1
    before = jnp.where(initial, outside, before)
    after = jnp.where(final, outside, after)
    previous = jnp.where(lane == 0, pltpu.roll(before, 65, 1), pltpu.roll(current, 1, 1))
    following = jnp.where(lane == 63, pltpu.roll(after, 63, 1), pltpu.roll(current, 127, 1))
    motion = link_ref[:, 0:128]
    motion_before = link_ref[:, 128:256]
    outside = pltpu.roll(first_edge_ref[:, 128:256], 65, 1)
    motion_before = jnp.where((lane == 0) & initial, outside, motion_before)
    ends = (lane[0:1] == 63) & final & (shard == shards - 1)
    starts = (lane[0:1] == 0) & initial & (shard == 0)
    weight_after = jnp.where(ends, 0.0, motion[6:7])
    weight_before = jnp.where(starts, 0.0, motion_before[6:7])
    scratch[0:8] = weight_before * (current - previous - motion_before) - weight_after * (
        following - current - motion
    )
    scratch[8:16] = sums
    scratch[16:24] = half_turn(sums)
    f = [scratch[8 + 8 * (q % 2) + q // 2 : 9 + 8 * (q % 2) + q // 2, :] for q in range(16)]
    g = [f[k] + scratch[k : k + 1, :] for k in range(6)]
    diagonal = weight_after + weight_before + damping
    s, c, m = f[6] + diagonal, f[7:10], f[10:16]
    inverse = 1.0 / s
    d = [c[k] * inverse for k in range(3)]
    n00 = m[1] + m[2] + diagonal - (c[1] * d[1] + c[2] * d[2])
    n11 = m[0] + m[2] + diagonal - (c[0] * d[0] + c[2] * d[2])
    n22 = m[0] + m[1] + diagonal - (c[0] * d[0] + c[1] * d[1])
    n01, n02, n12 = c[0] * d[1] - m[3], c[0] * d[2] - m[4], c[1] * d[2] - m[5]
    b0 = g[0] - (d[1] * g[5] - d[2] * g[4])
    b1 = g[1] - (d[2] * g[3] - d[0] * g[5])
    b2 = g[2] - (d[0] * g[4] - d[1] * g[3])
    x0, x1, x2 = solve3(n00, n11, n22, n01, n02, n12, b0, b1, b2)
    x3 = (g[3] + (c[1] * x2 - c[2] * x1)) * inverse
    x4 = (g[4] + (c[2] * x0 - c[0] * x2)) * inverse
    x5 = (g[5] + (c[0] * x1 - c[1] * x0)) * inverse
    for k, x in enumerate((x0, x1, x2, x3, x4, x5)):
        scratch[k : k + 1, :] = x
    return current - scratch[0:8]


def new_points(sums_ref, near_ref):
    x = [near_ref[0, :, 0:128], half_turn(near_ref[0, :, 0:128]), near_ref[0, :, 128:256]]
    q = []
    for k in range(5):
        pair = total(sums_ref, k * 8)
        q += [pair, half_turn(pair)]
    moved = solve3(q[0] + damping, q[1] + damping, q[2] + damping, -q[3], -q[4], -q[5], q[6], q[7], q[8])
    return [x[k] - moved[k] for k in range(3)]


def total(sums_ref, row):
    parts = [sums_ref[d, row : row + 8, :] for d in range(sums_ref.shape[0])]
    while len(parts) > 1:
        parts = [p + q for p, q in zip(parts[0::2], parts[1::2])]
    return parts[0]


def load_all(sources, targets, sems):
    loads = [pltpu.make_async_copy(a, b, sems.at[n]) for n, (a, b) in enumerate(zip(sources, targets))]
    for load in loads:
        load.start()
    return loads


def wait_all(loads):
    for load in loads:
        load.wait()


def update_kernel(sums_ref, near_hbm, link_hbm, edge_hbm, copies_ref, sent_hbm, *scratch):
    near_ref, link_ref, edge_ref, sent, scratch, sems = scratch
    loads = load_all([near_hbm, link_hbm, edge_hbm], [near_ref, link_ref, edge_ref], sems)
    frames = total(sums_ref, 40)
    wait_all(loads)
    lower = lanes((8, 128)) < 64
    pose = new_poses(frames, near_ref, link_ref, edge_ref, edge_ref, scratch)
    sent[...] = pose
    send = pltpu.make_async_copy(sent, sent_hbm, sems.at[3])
    send.start()
    x = new_points(sums_ref, near_ref)
    left = jnp.where(lower, x[0], half_turn(x[1]))
    right = jnp.where(lower, x[2], half_turn(pose))
    for d in range(copies_ref.shape[0]):
        copies_ref[d, :, 0:128] = left
        copies_ref[d, :, 128:256] = right
    send.wait()


def last_poses_kernel(sums_ref, near_hbm, link_hbm, edge_hbm, first_edge_hbm, copies_ref, *scratch):
    near_ref, link_ref, edge_ref, first_edge_ref, scratch, sems = scratch
    sources = [near_hbm, link_hbm, edge_hbm, first_edge_hbm]
    loads = load_all(sources, [near_ref, link_ref, edge_ref, first_edge_ref], sems)
    frames = total(sums_ref, 40)
    wait_all(loads)
    pose = new_poses(frames, near_ref, link_ref, edge_ref, first_edge_ref, scratch)
    lower = lanes((1, 128)) < 64
    for h in range(3):
        pair = jnp.where(lower, pose[2 * h : 2 * h + 1], half_turn(pose[2 * h + 1 : 2 * h + 2]))
        for d in range(copies_ref.shape[0]):
            copies_ref[d, :, h * 128 : (h + 1) * 128] = pair


def last_points_kernel(sums_ref, near_hbm, out_ref, near_ref, sem):
    load = pltpu.make_async_copy(near_hbm, near_ref, sem)
    load.start()
    load.wait()
    x = new_points(sums_ref, near_ref)
    for k in range(3):
        for b in range(8):
            out_ref[k : k + 1, b * 64 : (b + 1) * 64] = x[k][b : b + 1, 0:64]


def spread_kernel(poses_ref, out_ref):
    for d in range(poses_ref.shape[0]):
        for k in range(6):
            out_ref[k : k + 1, d * 64 : (d + 1) * 64] = poses_ref[d, :, k * 64 : (k + 1) * 64]


def call(kernel, outs, scratch, args, spaces, room=48):
    space = {"s": pltpu.SMEM, "v": pltpu.VMEM, "h": pltpu.HBM}
    specs = [pl.BlockSpec(memory_space=space[letter]) for letter in spaces]
    return pl.pallas_call(
        kernel,
        out_shape=outs,
        in_specs=specs[: len(args)],
        out_specs=specs[len(args) :],
        scratch_shapes=scratch,
        compiler_params=pltpu.CompilerParams(vmem_limit_bytes=67_043_328 - (room << 20)),
    )(*args)


def exchange(array):
    return lax.all_to_all(array, "lm", 0, 0, tiled=True)


def on_device(
    camera_poses,
    landmarks,
    odometry,
    odometry_info,
    observations,
    tile_frame,
    tile_block,
    tile_count,
    block_slot,
):
    owners, shards = lax.axis_size("lm"), lax.axis_size("tm")
    slots = observations.shape[0]
    f32 = jnp.float32
    seen = jnp.transpose(observations, (1, 2, 3, 0))
    to_edges = []
    for a in range(shards - 1):
        to_edges.append((a * owners + owners - 1, (a + 1) * owners))
        to_edges.append(((a + 1) * owners, a * owners + owners - 1))

    def edges(array):
        return lax.ppermute(array, ("tm", "lm"), to_edges)

    def shape(*sizes):
        return jax.ShapeDtypeStruct(sizes, f32)

    def buffer(*sizes):
        return pltpu.VMEM(sizes, f32)

    dma = pltpu.SemaphoreType.DMA
    names = jax.ShapeDtypeStruct((8, 128), jnp.int32)
    copies, sent, link, *names = call(
        pack_kernel,
        [shape(owners, 8, 256), shape(8, 256), shape(8, 256), names, names],
        [
            buffer(*landmarks.shape),
            buffer(*camera_poses.shape),
            buffer(*odometry.shape),
            buffer(1, camera_poses.shape[1]),
            pltpu.VMEM((1, slots), jnp.int32),
            pltpu.VMEM((1, slots), jnp.int32),
            pltpu.VMEM(block_slot.shape, jnp.int32),
            buffer(8, 1024),
            buffer(8, 256),
            buffer(8, 256),
            buffer(8, 256),
            pltpu.VMEM((8, 128), jnp.int32),
            dma((11 + owners,)),
        ],
        [
            tile_count,
            landmarks,
            camera_poses,
            odometry,
            odometry_info[None, :],
            tile_frame[None, :],
            tile_block[None, :],
            block_slot,
        ],
        "shhhhhhhhhhhh",
        0,
    )
    (folded,) = call(
        fold_kernel,
        [jax.ShapeDtypeStruct((3, PLAIN, TILE, 128), seen.dtype)],
        [
            pltpu.VMEM(seen.shape, seen.dtype),
            pltpu.VMEM((3, PLAIN, TILE, 128), seen.dtype),
            dma((1 + 2 * GROUPS,)),
        ],
        [seen],
        "hh",
        12,
    )
    first_edge = None
    for iteration in range(ITERS):
        window = exchange(copies)
        edge = edges(sent)
        sums, near = call(
            tiles_kernel,
            [shape(owners, 48, 128), shape(3, 8, 256)],
            [
                buffer(3, 8, 256),
                pltpu.VMEM(folded.shape, folded.dtype),
                buffer(6 * PLAIN, 128),
                buffer(GROUPS * 192, 128),
                buffer(1024, 128),
                buffer(576, 128),
                buffer(owners, 48, 128),
                dma((8,)),
                dma((6,)),
            ],
            [window, names[iteration], folded],
            "vvhhh",
            12,
        )
        sums = exchange(sums)
        if iteration == 0:
            first_edge = edge
            copies, sent = call(
                update_kernel,
                [shape(owners, 8, 256), shape(8, 128)],
                [buffer(3, 8, 256), buffer(8, 256), buffer(8, 256), buffer(8, 128), buffer(24, 128), dma((4,))],
                [sums, near, link, edge],
                "vhhhvh",
            )
    (copies,) = call(
        last_poses_kernel,
        [shape(owners, 1, 384)],
        [buffer(3, 8, 256), buffer(8, 256), buffer(8, 128), buffer(8, 256), buffer(24, 128), dma((4,))],
        [sums, near, link, edge, first_edge],
        "vhhhhv",
    )
    gathered = exchange(copies)
    (points,) = call(
        last_points_kernel, [shape(*landmarks.shape)], [buffer(3, 8, 256), dma], [sums, near], "vhv"
    )
    (poses,) = call(spread_kernel, [shape(*camera_poses.shape)], [], [gathered], "vv")
    return (poses, points)


def solution(mesh):
    return jax.shard_map(
        on_device,
        mesh=mesh,
        in_specs=(
            P(None, "tm"),
            P(None, ("tm", "lm")),
            P(None, "tm"),
            P("tm"),
            P(("tm", "lm"), None, None, None),
            P(("tm", "lm")),
            P(("tm", "lm")),
            P(("tm", "lm")),
            P("tm", None),
        ),
        out_specs=(P(None, "tm"), P(None, ("tm", "lm"))),
        check_vma=False,
    )
```

```python
import functools

import jax
import jax.numpy as jnp
from jax import lax
from jax.experimental import pallas as pl
from jax.experimental.pallas import tpu as pltpu
from jax.sharding import PartitionSpec as P

TILE = 64
ITERS = 2
SLOTS = 96
EXTRA = 128 - SLOTS
GROUPS = SLOTS // EXTRA
PLAIN = TILE * SLOTS // 128
FOLDED = TILE - PLAIN
PARTS = 2
damping = 1.0
scale = 4.0


def lanes(shape):
    return lax.broadcasted_iota(jnp.int32, shape, 1)


def half_turn(x):
    return pltpu.roll(x, 64, 1)


def own_block(ref, block):
    pair = jnp.zeros((8, 128), jnp.float32)
    for h in range(8):
        pair = jnp.where(block // 2 == h, ref[:, h * 128 : (h + 1) * 128], pair)
    return jnp.where(block % 2 == 1, half_turn(pair), pair)


def load_all(sources, targets, sems):
    loads = [pltpu.make_async_copy(a, b, sems.at[n]) for n, (a, b) in enumerate(zip(sources, targets))]
    for load in loads:
        load.start()
    return loads


def wait_all(loads):
    for load in loads:
        load.wait()


def pack_kernel(
    count_ref,
    points_hbm,
    poses_hbm,
    odometry_hbm,
    info_hbm,
    frame_hbm,
    block_hbm,
    slot_hbm,
    copies_hbm,
    edge_hbm,
    link_hbm,
    names_hbm,
    more_names_hbm,
    points,
    poses,
    odometry,
    info,
    frame,
    block,
    slot,
    rows,
    chunk,
    edge,
    link_ref,
    names_ref,
    sems,
):
    loads = [
        pltpu.make_async_copy(source, target, sems.at[n])
        for n, (source, target) in enumerate(
            [
                (poses_hbm, poses),
                (points_hbm, points),
                (odometry_hbm, odometry),
                (info_hbm, info),
                (frame_hbm, frame),
                (block_hbm, block),
                (slot_hbm, slot),
            ]
        )
    ]
    for load in loads:
        load.start()
    rows[...] = jnp.zeros((8, 1024), jnp.float32)
    owner = lax.axis_index("lm")
    lane = lanes((8, 128))
    for load in loads:
        load.wait()
    rows[0:6, :] = poses[...]
    pose = own_block(rows, owner)
    for k in range(3):
        for b in range(8):
            chunk[b : b + 1, k * 64 : (k + 1) * 64] = points[k : k + 1, b * 64 : (b + 1) * 64]
    chunk[:, 192:256] = half_turn(pose)[:, 64:128]
    owners = copies_hbm.shape[0]
    sends = [pltpu.make_async_copy(chunk, copies_hbm.at[d], sems.at[10 + d]) for d in range(owners)]
    for send in sends:
        send.start()
    rows[0:6, :] = odometry[...]
    rows[6:7, :] = info[...]
    current = own_block(rows, owner)
    before = own_block(rows, owner - 1)
    edge[:, 0:128] = pose
    edge[:, 128:256] = current
    sends.append(pltpu.make_async_copy(edge, edge_hbm, sems.at[7]))
    sends[-1].start()
    link_ref[:, 0:128] = current
    link_ref[:, 128:256] = jnp.where(lane == 0, pltpu.roll(before, 65, 1), pltpu.roll(current, 1, 1))
    sends.append(pltpu.make_async_copy(link_ref, link_hbm, sems.at[8]))
    sends[-1].start()
    slots = frame.shape[1]
    row = lax.broadcasted_iota(jnp.int32, (128, slots), 0)
    named = jnp.where(block[...] == row, 1.0, 0.0).astype(jnp.bfloat16)
    table = jnp.broadcast_to(slot[...].astype(jnp.float32), (8, 128)).astype(jnp.bfloat16)
    position = dot(table, named)[0:1].astype(jnp.int32)
    live = lanes((1, slots)) < count_ref[0]
    names_ref[...] = jnp.full(names_ref.shape, -1, jnp.int32)
    names_ref[0:1, 0:slots] = jnp.where(live, frame[...], -1)
    names_ref[1:2, 0:slots] = jnp.where(live, position, -1)
    for n in range(2):
        name = names_ref[...][n : n + 1]
        for g in range(GROUPS):
            folded = jnp.where(lane[0:1] < SLOTS, name, pltpu.roll(name, SLOTS - g * EXTRA, 1))
            names_ref[2 + n * GROUPS + g : 3 + n * GROUPS + g, :] = folded
    sends.append(pltpu.make_async_copy(names_ref, names_hbm, sems.at[9]))
    sends[-1].start()
    sends.append(pltpu.make_async_copy(names_ref, more_names_hbm, sems.at[10 + owners]))
    sends[-1].start()
    for send in sends:
        send.wait()


def split(x, parts):
    pieces = []
    for _ in range(parts - 1):
        pieces.append(x.astype(jnp.bfloat16))
        x = x - pieces[-1].astype(jnp.float32)
    pieces.append(x.astype(jnp.bfloat16))
    return pieces


def dot(a, b):
    return lax.dot_general(a, b, (((1,), (0,)), ((), ())), preferred_element_type=jnp.float32)


def dot_t(a, b):
    return lax.dot_general(a, b, (((1,), (1,)), ((), ())), preferred_element_type=jnp.float32)


def fold_kernel(seen_hbm, folded, seen, sems):
    parts = [pl.ds(PLAIN, FOLDED)] + [pl.ds(g * FOLDED, FOLDED) for g in range(GROUPS)]
    loads = [
        pltpu.make_async_copy(seen_hbm.at[:, part], seen.at[:, part], sems.at[n]) for n, part in enumerate(parts)
    ]
    for load in loads:
        load.start()
    loads[0].wait()
    for g in range(GROUPS):
        loads[1 + g].wait()

        def step(m, carry):
            for k in range(3):
                for r in range(0, TILE, 16):
                    wide = seen[k, g * FOLDED + m, r : r + 16, :]
                    more = seen[k, PLAIN + m, r : r + 16, g * EXTRA : (g + 1) * EXTRA]
                    folded[k, g * FOLDED + m, r : r + 16, :] = jnp.concatenate([wide, more], axis=1)
            return carry

        lax.fori_loop(0, FOLDED, step, 0)


def unfold(parts):
    lane = lanes(parts.shape[1:])
    result = jnp.where(lane < SLOTS, sum(parts[g] for g in range(GROUPS)), 0.0)
    for g in range(GROUPS):
        mine = (lane >= g * EXTRA) & (lane < (g + 1) * EXTRA)
        result = result + jnp.where(mine, pltpu.roll(parts[g], (g + 1) * EXTRA, 1), 0.0)
    return result


def tiles_kernel(window_ref, names_ref, seen_ref, out_hbm, near_hbm, *scratch):
    near_ref, pose, point, fsum, psum, partial, right, sums, sems = scratch
    owner, owners = lax.axis_index("lm"), lax.axis_size("lm")
    near_ref[0] = window_ref[owner]
    near_ref[1] = window_ref[jnp.maximum(owner - 1, 0)]
    near_ref[2] = window_ref[jnp.minimum(owner + 1, owners - 1)]
    turned = split(jnp.transpose(window_ref[...].reshape(128, 256), (1, 0)), PARTS)
    put_near = pltpu.make_async_copy(near_ref, near_hbm, sems.at[7])
    put_near.start()
    row = lax.broadcasted_iota(jnp.int32, (128, 128), 0)
    lane = lanes((FOLDED, 128))
    points = jnp.concatenate([piece[0:192] for piece in turned], axis=0)
    for g in range(GROUPS):
        frame, position = names_ref[2 + g : 3 + g, :], names_ref[2 + GROUPS + g : 3 + GROUPS + g, :]
        pick = jnp.where(position == row, 1.0, 0.0).astype(jnp.bfloat16)
        found = dot(points, pick)
        point[g * 192 : (g + 1) * 192, :] = sum(found[n * 192 : (n + 1) * 192] for n in range(PARTS))
        at = 192 + g * FOLDED
        poses = jnp.concatenate(
            [piece[r : r + FOLDED] for r in (at, 192 + PLAIN) for piece in turned], axis=0
        )
        for k in range(6):
            pick = jnp.where(frame * 8 + k == row, 1.0, 0.0).astype(jnp.bfloat16)
            both = dot(poses, pick)
            found = [both[n * FOLDED : (n + 1) * FOLDED] for n in range(2 * PARTS)]
            found = [sum(found[:PARTS]), sum(found[PARTS:])]
            pose[k * PLAIN + g * FOLDED : k * PLAIN + (g + 1) * FOLDED, :] = jnp.where(lane < SLOTS, *found)
    psum[...] = jnp.zeros_like(psum)
    partial[...] = jnp.zeros_like(partial)

    sub = lax.broadcasted_iota(jnp.int32, (8, 128), 0)

    def merge(a, b, shift):
        low = (sub // shift) % 2 == 0
        if shift == 4:
            return jnp.where(low, a, b) + pltpu.roll(jnp.where(low, b, a), 4, 0)
        return jnp.where(low, a + pltpu.roll(a, 8 - shift, 0), b + pltpu.roll(b, shift, 0))

    def finish(i):
        for half in range(2):
            parts = [partial[(half * 8 + q) * 8 : (half * 8 + q + 1) * 8, :] for q in range(8)]
            for shift in (4, 2, 1):
                count = len(parts) // 2
                parts = [merge(parts[q], parts[q + count], shift) for q in range(count)]
            fsum[pl.ds(pl.multiple_of(i * 16 + half * 8, 8), 8), :] = parts[0]

    def step(g, i, carry):
        finish(jnp.maximum(i - 1, 0))
        w = [jnp.broadcast_to(pose[pl.ds(k * PLAIN + i, 1), :], (8, 128)) for k in range(3)]
        t = [jnp.broadcast_to(pose[pl.ds((3 + k) * PLAIN + i, 1), :], (8, 128)) for k in range(3)]
        w00, w11, w22 = w[0] * w[0], w[1] * w[1], w[2] * w[2]
        m00, m11, m22 = 1.0 + (w11 + w22), 1.0 + (w00 + w22), 1.0 + (w00 + w11)
        m01, m02, m12 = w[0] * w[1], w[0] * w[2], w[1] * w[2]
        total = [None] * 16
        for part in range(0, TILE, 16):
            seen = [seen_ref[k, i, part : part + 16, :].astype(jnp.float32) for k in range(3)]
            for h in range(2):
                at = part + h * 8
                x = [point[(g * 3 + k) * 64 + at : (g * 3 + k) * 64 + at + 8, :] for k in range(3)]
                o = [seen[k][h * 8 : (h + 1) * 8] for k in range(3)]
                r0 = (x[0] + t[0] - o[0]) + (w[1] * x[2] - w[2] * x[1])
                r1 = (x[1] + t[1] - o[1]) + (w[2] * x[0] - w[0] * x[2])
                r2 = (x[2] + t[2] - o[2]) + (w[0] * x[1] - w[1] * x[0])
                c = 1.0 / (scale + (r0 * r0 + r1 * r1 + r2 * r2))
                c0, c1, c2 = c * r0, c * r1, c * r2
                y = [c * x[k] for k in range(3)]
                terms = [
                    x[1] * c2 - x[2] * c1,
                    x[2] * c0 - x[0] * c2,
                    x[0] * c1 - x[1] * c0,
                    c0,
                    c1,
                    c2,
                    c,
                    y[0],
                    y[1],
                    y[2],
                    y[0] * x[0],
                    y[1] * x[1],
                    y[2] * x[2],
                    y[0] * x[1],
                    y[0] * x[2],
                    y[1] * x[2],
                ]
                total = terms if total[0] is None else [p + q for p, q in zip(total, terms)]
                terms = [
                    c * m00,
                    c * m11,
                    c * m22,
                    c * m01,
                    c * m02,
                    c * m12,
                    c0 - (w[1] * c2 - w[2] * c1),
                    c1 - (w[2] * c0 - w[0] * c2),
                    c2 - (w[0] * c1 - w[1] * c0),
                ]
                for q, term in enumerate(terms):
                    psum[g, q * 64 + at : q * 64 + at + 8, :] += term
        for q in range(16):
            partial[q * 8 : (q + 1) * 8, :] = total[q]
        return carry

    for g in range(GROUPS):
        lax.fori_loop(g * FOLDED, (g + 1) * FOLDED, functools.partial(step, g), 0)
    finish(PLAIN - 1)
    frame_sums = []
    for q in range(16):
        rows = fsum[pl.ds(q, PLAIN, stride=16), :]
        back = jnp.zeros((FOLDED, 128), jnp.float32)
        for g in range(GROUPS):
            mine = (lane >= g * EXTRA) & (lane < (g + 1) * EXTRA)
            back = jnp.where(mine, pltpu.roll(rows[g * FOLDED : (g + 1) * FOLDED], (g + 1) * EXTRA, 1), back)
        frame_sums += [rows, back]
    frame, position = names_ref[0:1, :], names_ref[1:2, :]
    held = position == row
    own = jnp.where(frame == lax.broadcasted_iota(jnp.int32, (16, 128), 0), scale, 0.0).astype(jnp.bfloat16)
    frames = sum(dot_t(own, piece) for piece in split(jnp.concatenate(frame_sums, axis=0), PARTS))
    for r in range(4):
        pair = frames[:, r * 128 : (r + 1) * 128]
        right[:, 2 * r, :] = half_turn(pair)
        right[:, 2 * r + 1, :] = pair
        sums[:, 10, r, :] = frames[:, (4 + r) * 128 : (5 + r) * 128]
    put_near.wait()
    stores = [pltpu.make_async_copy(sums.at[:, 10], out_hbm.at[:, 10], sems.at[5])]
    stores[0].start()
    own = jnp.where(held, scale, 0.0).astype(jnp.bfloat16)
    for q in range(5):
        wide = 128 if q < 4 else 64
        part = unfold(psum[:, q * 128 : q * 128 + wide, :])
        part = sum(dot_t(own, piece) for piece in split(part, PARTS))
        if wide < 128:
            part = jnp.concatenate([part, jnp.zeros_like(part)], axis=1)
        part = part.reshape(16, 8, 128)
        if wide < 128:
            part = jnp.where(lax.broadcasted_iota(jnp.int32, part.shape, 2) < 64, part, right[...])
        sums[:, 2 * q] = part[:, 0:4]
        sums[:, 2 * q + 1] = part[:, 4:8]
        rows = slice(2 * q, 2 * q + 2)
        stores.append(pltpu.make_async_copy(sums.at[:, rows], out_hbm.at[:, rows], sems.at[q]))
        stores[-1].start()
    wait_all(stores)


def solve3(m00, m11, m22, m01, m02, m12, b0, b1, b2):
    i0 = 1.0 / m00
    l1, l2 = m01 * i0, m02 * i0
    d1 = m11 - l1 * m01
    e = m12 - l1 * m02
    i1 = 1.0 / d1
    l3 = e * i1
    d2 = m22 - l2 * m02 - l3 * e
    y1 = b1 - l1 * b0
    y2 = b2 - l2 * b0 - l3 * y1
    x2 = y2 / d2
    x1 = y1 * i1 - l3 * x2
    x0 = b0 * i0 - l1 * x1 - l2 * x2
    return x0, x1, x2


def new_poses(lower_sums, upper_sums, near_ref, link_ref, edge_ref, first_edge_ref, scratch):
    owner, shard = lax.axis_index("lm"), lax.axis_index("tm")
    owners, shards = lax.axis_size("lm"), lax.axis_size("tm")
    lane = lanes((8, 128))
    current, before, after = (half_turn(near_ref[n, :, 128:256]) for n in range(3))
    outside = edge_ref[:, 0:128]
    initial, final = owner == 0, owner == owners - 1
    before = jnp.where(initial, outside, before)
    after = jnp.where(final, outside, after)
    previous = jnp.where(lane == 0, pltpu.roll(before, 65, 1), pltpu.roll(current, 1, 1))
    following = jnp.where(lane == 63, pltpu.roll(after, 63, 1), pltpu.roll(current, 127, 1))
    motion = link_ref[:, 0:128]
    motion_before = link_ref[:, 128:256]
    outside = pltpu.roll(first_edge_ref[:, 128:256], 65, 1)
    motion_before = jnp.where((lane == 0) & initial, outside, motion_before)
    ends = (lane[0:1] == 63) & final & (shard == shards - 1)
    starts = (lane[0:1] == 0) & initial & (shard == 0)
    weight_after = jnp.where(ends, 0.0, motion[6:7])
    weight_before = jnp.where(starts, 0.0, motion_before[6:7])
    scratch[0:8] = weight_before * (current - previous - motion_before) - weight_after * (
        following - current - motion
    )
    scratch[8:16] = half_turn(lower_sums)
    scratch[16:20] = upper_sums
    scratch[20:24] = half_turn(upper_sums)
    f = [scratch[8 + q : 9 + q, :] for q in range(8)]
    for r in range(4):
        f += [scratch[16 + r : 17 + r, :], scratch[20 + r : 21 + r, :]]
    g = [f[k] + scratch[k : k + 1, :] for k in range(6)]
    diagonal = weight_after + weight_before + damping
    s, c, m = f[6] + diagonal, f[7:10], f[10:16]
    inverse = 1.0 / s
    d = [c[k] * inverse for k in range(3)]
    n00 = m[1] + m[2] + diagonal - (c[1] * d[1] + c[2] * d[2])
    n11 = m[0] + m[2] + diagonal - (c[0] * d[0] + c[2] * d[2])
    n22 = m[0] + m[1] + diagonal - (c[0] * d[0] + c[1] * d[1])
    n01, n02, n12 = c[0] * d[1] - m[3], c[0] * d[2] - m[4], c[1] * d[2] - m[5]
    b0 = g[0] - (d[1] * g[5] - d[2] * g[4])
    b1 = g[1] - (d[2] * g[3] - d[0] * g[5])
    b2 = g[2] - (d[0] * g[4] - d[1] * g[3])
    x0, x1, x2 = solve3(n00, n11, n22, n01, n02, n12, b0, b1, b2)
    x3 = (g[3] + (c[1] * x2 - c[2] * x1)) * inverse
    x4 = (g[4] + (c[2] * x0 - c[0] * x2)) * inverse
    x5 = (g[5] + (c[0] * x1 - c[1] * x0)) * inverse
    for k, x in enumerate((x0, x1, x2, x3, x4, x5)):
        scratch[k : k + 1, :] = x
    return current - scratch[0:8]


def new_points(sums, near_ref):
    x = [near_ref[0, :, 0:128], half_turn(near_ref[0, :, 0:128]), near_ref[0, :, 128:256]]
    q = []
    for pair in sums:
        q += [pair, half_turn(pair)]
    moved = solve3(q[0] + damping, q[1] + damping, q[2] + damping, -q[3], -q[4], -q[5], q[6], q[7], q[8])
    return [x[k] - moved[k] for k in range(3)]


def total(sums_ref, part):
    parts = [sums_ref[d, part] for d in range(sums_ref.shape[0])]
    while len(parts) > 1:
        parts = [p + q for p, q in zip(parts[0::2], parts[1::2])]
    return parts[0]


def pair_total(sums_ref, k):
    return jnp.concatenate([total(sums_ref, 2 * k), total(sums_ref, 2 * k + 1)], axis=0)


def update_kernel(sums_ref, near_hbm, link_hbm, edge_hbm, copies_ref, sent_hbm, *scratch):
    near_ref, link_ref, edge_ref, sent, scratch, sems = scratch
    loads = load_all([near_hbm, link_hbm, edge_hbm], [near_ref, link_ref, edge_ref], sems)
    frames = pair_total(sums_ref, 4), total(sums_ref, 10)
    wait_all(loads)
    lower = lanes((8, 128)) < 64
    pose = new_poses(*frames, near_ref, link_ref, edge_ref, edge_ref, scratch)
    sent[...] = pose
    send = pltpu.make_async_copy(sent, sent_hbm, sems.at[3])
    send.start()
    x = new_points([pair_total(sums_ref, k) for k in range(4)] + [frames[0]], near_ref)
    left = jnp.where(lower, x[0], half_turn(x[1]))
    right = jnp.where(lower, x[2], half_turn(pose))
    for d in range(copies_ref.shape[0]):
        copies_ref[d, :, 0:128] = left
        copies_ref[d, :, 128:256] = right
    send.wait()


def last_poses_kernel(sums_ref, near_hbm, link_hbm, edge_hbm, first_edge_hbm, copies_ref, *scratch):
    near_ref, link_ref, edge_ref, first_edge_ref, scratch, sems = scratch
    sources = [near_hbm, link_hbm, edge_hbm, first_edge_hbm]
    loads = load_all(sources, [near_ref, link_ref, edge_ref, first_edge_ref], sems)
    frames = pair_total(sums_ref, 4), total(sums_ref, 10)
    wait_all(loads)
    pose = new_poses(*frames, near_ref, link_ref, edge_ref, first_edge_ref, scratch)
    lower = lanes((1, 128)) < 64
    for h in range(3):
        pair = jnp.where(lower, pose[2 * h : 2 * h + 1], half_turn(pose[2 * h + 1 : 2 * h + 2]))
        for d in range(copies_ref.shape[0]):
            copies_ref[d, :, h * 128 : (h + 1) * 128] = pair


def last_points_kernel(sums_ref, near_hbm, out_ref, near_ref, sem):
    load = pltpu.make_async_copy(near_hbm, near_ref, sem)
    load.start()
    sums = [pair_total(sums_ref, k) for k in range(5)]
    load.wait()
    x = new_points(sums, near_ref)
    for k in range(3):
        for b in range(8):
            out_ref[k : k + 1, b * 64 : (b + 1) * 64] = x[k][b : b + 1, 0:64]


def spread_kernel(poses_ref, out_ref):
    for d in range(poses_ref.shape[0]):
        for k in range(6):
            out_ref[k : k + 1, d * 64 : (d + 1) * 64] = poses_ref[d, :, k * 64 : (k + 1) * 64]


def call(kernel, outs, scratch, args, spaces, room=48):
    space = {"s": pltpu.SMEM, "v": pltpu.VMEM, "h": pltpu.HBM}
    specs = [pl.BlockSpec(memory_space=space[letter]) for letter in spaces]
    return pl.pallas_call(
        kernel,
        out_shape=outs,
        in_specs=specs[: len(args)],
        out_specs=specs[len(args) :],
        scratch_shapes=scratch,
        compiler_params=pltpu.CompilerParams(vmem_limit_bytes=67_043_328 - (room << 20)),
    )(*args)


def exchange(array):
    return lax.all_to_all(array, "lm", 0, 0, tiled=True)


def on_device(
    camera_poses,
    landmarks,
    odometry,
    odometry_info,
    observations,
    tile_frame,
    tile_block,
    tile_count,
    block_slot,
):
    owners, shards = lax.axis_size("lm"), lax.axis_size("tm")
    slots = observations.shape[0]
    f32 = jnp.float32
    seen = jnp.transpose(observations, (1, 2, 3, 0))
    to_edges = []
    for a in range(shards - 1):
        to_edges.append((a * owners + owners - 1, (a + 1) * owners))
        to_edges.append(((a + 1) * owners, a * owners + owners - 1))

    def edges(array):
        return lax.ppermute(array, ("tm", "lm"), to_edges)

    def shape(*sizes):
        return jax.ShapeDtypeStruct(sizes, f32)

    def buffer(*sizes):
        return pltpu.VMEM(sizes, f32)

    dma = pltpu.SemaphoreType.DMA
    names = jax.ShapeDtypeStruct((8, 128), jnp.int32)
    copies, sent, link, *names = call(
        pack_kernel,
        [shape(owners, 8, 256), shape(8, 256), shape(8, 256), names, names],
        [
            buffer(*landmarks.shape),
            buffer(*camera_poses.shape),
            buffer(*odometry.shape),
            buffer(1, camera_poses.shape[1]),
            pltpu.VMEM((1, slots), jnp.int32),
            pltpu.VMEM((1, slots), jnp.int32),
            pltpu.VMEM(block_slot.shape, jnp.int32),
            buffer(8, 1024),
            buffer(8, 256),
            buffer(8, 256),
            buffer(8, 256),
            pltpu.VMEM((8, 128), jnp.int32),
            dma((11 + owners,)),
        ],
        [
            tile_count,
            landmarks,
            camera_poses,
            odometry,
            odometry_info[None, :],
            tile_frame[None, :],
            tile_block[None, :],
            block_slot,
        ],
        "shhhhhhhhhhhh",
        0,
    )
    (folded,) = call(
        fold_kernel,
        [jax.ShapeDtypeStruct((3, PLAIN, TILE, 128), seen.dtype)],
        [
            pltpu.VMEM(seen.shape, seen.dtype),
            dma((1 + GROUPS,)),
        ],
        [seen],
        "hv",
        14,
    )
    first_edge = None
    for iteration in range(ITERS):
        window = exchange(copies)
        edge = edges(sent)
        sums, near = call(
            tiles_kernel,
            [shape(owners, 11, 4, 128), shape(3, 8, 256)],
            [
                buffer(3, 8, 256),
                buffer(6 * PLAIN, 128),
                buffer(GROUPS * 192, 128),
                buffer(16 * PLAIN, 128),
                buffer(GROUPS, 576, 128),
                buffer(128, 128),
                buffer(owners, 8, 128),
                buffer(owners, 11, 4, 128),
                dma((8,)),
            ],
            [window, names[iteration], folded],
            "vvvhh",
            14,
        )
        sums = exchange(sums)
        if iteration == 0:
            first_edge = edge
            copies, sent = call(
                update_kernel,
                [shape(owners, 8, 256), shape(8, 128)],
                [buffer(3, 8, 256), buffer(8, 256), buffer(8, 256), buffer(8, 128), buffer(24, 128), dma((4,))],
                [sums, near, link, edge],
                "vhhhvh",
            )
    (copies,) = call(
        last_poses_kernel,
        [shape(owners, 1, 384)],
        [buffer(3, 8, 256), buffer(8, 256), buffer(8, 128), buffer(8, 256), buffer(24, 128), dma((4,))],
        [sums, near, link, edge, first_edge],
        "vhhhhv",
    )
    gathered = exchange(copies)
    (points,) = call(
        last_points_kernel, [shape(*landmarks.shape)], [buffer(3, 8, 256), dma], [sums, near], "vhv"
    )
    (poses,) = call(spread_kernel, [shape(*camera_poses.shape)], [], [gathered], "vv")
    return (poses, points)


def solution(mesh):
    return jax.shard_map(
        on_device,
        mesh=mesh,
        in_specs=(
            P(None, "tm"),
            P(None, ("tm", "lm")),
            P(None, "tm"),
            P("tm"),
            P(("tm", "lm"), None, None, None),
            P(("tm", "lm")),
            P(("tm", "lm")),
            P(("tm", "lm")),
            P("tm", None),
        ),
        out_specs=(P(None, "tm"), P(None, ("tm", "lm"))),
        check_vma=False,
    )
```

```python
import functools

import jax
import jax.numpy as jnp
from jax import lax
from jax.experimental import pallas as pl
from jax.experimental.pallas import tpu as pltpu
from jax.sharding import PartitionSpec as P

TILE = 64
ITERS = 2
SLOTS = 96
EXTRA = 128 - SLOTS
GROUPS = SLOTS // EXTRA
PLAIN = TILE * SLOTS // 128
FOLDED = TILE - PLAIN
PARTS = 2
damping = 1.0
scale = 4.0


def lanes(shape):
    return lax.broadcasted_iota(jnp.int32, shape, 1)


def half_turn(x):
    return pltpu.roll(x, 64, 1)


def own_frames():
    owners = lax.axis_size("lm")
    return lax.rem(lax.axis_index("lm") + owners // 2 - 1, owners)


def own_block(ref, block):
    pair = jnp.zeros((8, 128), jnp.float32)
    for h in range(8):
        pair = jnp.where(block // 2 == h, ref[:, h * 128 : (h + 1) * 128], pair)
    return jnp.where(block % 2 == 1, half_turn(pair), pair)


def load_all(sources, targets, sems):
    loads = [pltpu.make_async_copy(a, b, sems.at[n]) for n, (a, b) in enumerate(zip(sources, targets))]
    for load in loads:
        load.start()
    return loads


def wait_all(loads):
    for load in loads:
        load.wait()


def pack_kernel(
    count_ref,
    points_hbm,
    poses_hbm,
    odometry_hbm,
    info_hbm,
    frame_hbm,
    block_hbm,
    slot_hbm,
    copies_hbm,
    edge_hbm,
    link_hbm,
    names_hbm,
    more_names_hbm,
    points,
    poses,
    odometry,
    info,
    frame,
    block,
    slot,
    rows,
    chunk,
    edge,
    link_ref,
    names_ref,
    sems,
):
    loads = [
        pltpu.make_async_copy(source, target, sems.at[n])
        for n, (source, target) in enumerate(
            [
                (poses_hbm, poses),
                (points_hbm, points),
                (odometry_hbm, odometry),
                (info_hbm, info),
                (frame_hbm, frame),
                (block_hbm, block),
                (slot_hbm, slot),
            ]
        )
    ]
    for load in loads:
        load.start()
    rows[...] = jnp.zeros((8, 1024), jnp.float32)
    block_of_frames = own_frames()
    lane = lanes((8, 128))
    for load in loads:
        load.wait()
    rows[0:6, :] = poses[...]
    pose = own_block(rows, block_of_frames)
    for k in range(3):
        for b in range(8):
            chunk[b : b + 1, k * 64 : (k + 1) * 64] = points[k : k + 1, b * 64 : (b + 1) * 64]
    chunk[:, 192:256] = half_turn(pose)[:, 64:128]
    owners = copies_hbm.shape[0]
    sends = [pltpu.make_async_copy(chunk, copies_hbm.at[d], sems.at[10 + d]) for d in range(owners)]
    for send in sends:
        send.start()
    rows[0:6, :] = odometry[...]
    rows[6:7, :] = info[...]
    current = own_block(rows, block_of_frames)
    before = own_block(rows, block_of_frames - 1)
    edge[:, 0:128] = pose
    edge[:, 128:256] = current
    sends.append(pltpu.make_async_copy(edge, edge_hbm, sems.at[7]))
    sends[-1].start()
    link_ref[:, 0:128] = current
    link_ref[:, 128:256] = jnp.where(lane == 0, pltpu.roll(before, 65, 1), pltpu.roll(current, 1, 1))
    sends.append(pltpu.make_async_copy(link_ref, link_hbm, sems.at[8]))
    sends[-1].start()
    slots = frame.shape[1]
    row = lax.broadcasted_iota(jnp.int32, (128, slots), 0)
    named = jnp.where(block[...] == row, 1.0, 0.0).astype(jnp.bfloat16)
    table = jnp.broadcast_to(slot[...].astype(jnp.float32), (8, 128)).astype(jnp.bfloat16)
    position = dot(table, named)[0:1].astype(jnp.int32)
    live = lanes((1, slots)) < count_ref[0]
    names_ref[...] = jnp.full(names_ref.shape, -1, jnp.int32)
    names_ref[0:1, 0:slots] = jnp.where(live, (frame[...] + owners // 2 + 1) & (owners - 1), -1)
    names_ref[1:2, 0:slots] = jnp.where(live, position, -1)
    for n in range(2):
        name = names_ref[...][n : n + 1]
        for g in range(GROUPS):
            folded = jnp.where(lane[0:1] < SLOTS, name, pltpu.roll(name, SLOTS - g * EXTRA, 1))
            names_ref[2 + n * GROUPS + g : 3 + n * GROUPS + g, :] = folded
    sends.append(pltpu.make_async_copy(names_ref, names_hbm, sems.at[9]))
    sends[-1].start()
    sends.append(pltpu.make_async_copy(names_ref, more_names_hbm, sems.at[10 + owners]))
    sends[-1].start()
    for send in sends:
        send.wait()


def split(x, parts):
    pieces = []
    for _ in range(parts - 1):
        pieces.append(x.astype(jnp.bfloat16))
        x = x - pieces[-1].astype(jnp.float32)
    pieces.append(x.astype(jnp.bfloat16))
    return pieces


def dot(a, b):
    return lax.dot_general(a, b, (((1,), (0,)), ((), ())), preferred_element_type=jnp.float32)


def dot_t(a, b):
    return lax.dot_general(a, b, (((1,), (1,)), ((), ())), preferred_element_type=jnp.float32)


def fold_kernel(seen_hbm, folded, seen, sems):
    parts = [pl.ds(PLAIN, FOLDED)] + [pl.ds(g * FOLDED, FOLDED) for g in range(GROUPS)]
    loads = [
        pltpu.make_async_copy(seen_hbm.at[:, part], seen.at[:, part], sems.at[n]) for n, part in enumerate(parts)
    ]
    for load in loads:
        load.start()
    loads[0].wait()
    for g in range(GROUPS):
        loads[1 + g].wait()

        def step(m, carry):
            for k in range(3):
                for r in range(0, TILE, 16):
                    wide = seen[k, g * FOLDED + m, r : r + 16, :]
                    more = seen[k, PLAIN + m, r : r + 16, g * EXTRA : (g + 1) * EXTRA]
                    folded[k, g * FOLDED + m, r : r + 16, :] = jnp.concatenate([wide, more], axis=1)
            return carry

        lax.fori_loop(0, FOLDED, step, 0)


def unfold(parts):
    lane = lanes(parts.shape[1:])
    result = jnp.where(lane < SLOTS, sum(parts[g] for g in range(GROUPS)), 0.0)
    for g in range(GROUPS):
        mine = (lane >= g * EXTRA) & (lane < (g + 1) * EXTRA)
        result = result + jnp.where(mine, pltpu.roll(parts[g], (g + 1) * EXTRA, 1), 0.0)
    return result


def tiles_kernel(window_ref, names_ref, seen_ref, out_hbm, near_hbm, *scratch):
    near_ref, pose, point, fsum, psum, partial, right, sums, sems = scratch
    owner, owners = lax.axis_index("lm"), lax.axis_size("lm")
    near_ref[0] = window_ref[owner]
    near_ref[1] = window_ref[lax.rem(owner + owners - 1, owners)]
    near_ref[2] = window_ref[lax.rem(owner + 1, owners)]
    turned = split(jnp.transpose(window_ref[...].reshape(128, 256), (1, 0)), PARTS)
    put_near = pltpu.make_async_copy(near_ref, near_hbm, sems.at[7])
    put_near.start()
    row = lax.broadcasted_iota(jnp.int32, (128, 128), 0)
    lane = lanes((FOLDED, 128))
    points = jnp.concatenate([piece[0:192] for piece in turned], axis=0)
    for g in range(GROUPS):
        frame, position = names_ref[2 + g : 3 + g, :], names_ref[2 + GROUPS + g : 3 + GROUPS + g, :]
        pick = jnp.where(position == row, 1.0, 0.0).astype(jnp.bfloat16)
        found = dot(points, pick)
        point[g * 192 : (g + 1) * 192, :] = sum(found[n * 192 : (n + 1) * 192] for n in range(PARTS))
        at = 192 + g * FOLDED
        poses = jnp.concatenate(
            [piece[r : r + FOLDED] for r in (at, 192 + PLAIN) for piece in turned], axis=0
        )
        for k in range(6):
            pick = jnp.where(frame * 8 + k == row, 1.0, 0.0).astype(jnp.bfloat16)
            both = dot(poses, pick)
            found = [both[n * FOLDED : (n + 1) * FOLDED] for n in range(2 * PARTS)]
            found = [sum(found[:PARTS]), sum(found[PARTS:])]
            pose[k * PLAIN + g * FOLDED : k * PLAIN + (g + 1) * FOLDED, :] = jnp.where(lane < SLOTS, *found)
    psum[...] = jnp.zeros_like(psum)
    partial[...] = jnp.zeros_like(partial)

    sub = lax.broadcasted_iota(jnp.int32, (8, 128), 0)

    def merge(a, b, shift):
        low = (sub // shift) % 2 == 0
        if shift == 4:
            return jnp.where(low, a, b) + pltpu.roll(jnp.where(low, b, a), 4, 0)
        return jnp.where(low, a + pltpu.roll(a, 8 - shift, 0), b + pltpu.roll(b, shift, 0))

    def finish(i):
        for half in range(2):
            parts = [partial[(half * 8 + q) * 8 : (half * 8 + q + 1) * 8, :] for q in range(8)]
            for shift in (4, 2, 1):
                count = len(parts) // 2
                parts = [merge(parts[q], parts[q + count], shift) for q in range(count)]
            fsum[pl.ds(pl.multiple_of(i * 16 + half * 8, 8), 8), :] = parts[0]

    def step(g, i, carry):
        finish(jnp.maximum(i - 1, 0))
        w = [jnp.broadcast_to(pose[pl.ds(k * PLAIN + i, 1), :], (8, 128)) for k in range(3)]
        t = [jnp.broadcast_to(pose[pl.ds((3 + k) * PLAIN + i, 1), :], (8, 128)) for k in range(3)]
        w00, w11, w22 = w[0] * w[0], w[1] * w[1], w[2] * w[2]
        m00, m11, m22 = 1.0 + (w11 + w22), 1.0 + (w00 + w22), 1.0 + (w00 + w11)
        m01, m02, m12 = w[0] * w[1], w[0] * w[2], w[1] * w[2]
        total = [None] * 16
        for part in range(0, TILE, 16):
            seen = [seen_ref[k, i, part : part + 16, :].astype(jnp.float32) for k in range(3)]
            for h in range(2):
                at = part + h * 8
                x = [point[(g * 3 + k) * 64 + at : (g * 3 + k) * 64 + at + 8, :] for k in range(3)]
                o = [seen[k][h * 8 : (h + 1) * 8] for k in range(3)]
                r0 = (x[0] + t[0] - o[0]) + (w[1] * x[2] - w[2] * x[1])
                r1 = (x[1] + t[1] - o[1]) + (w[2] * x[0] - w[0] * x[2])
                r2 = (x[2] + t[2] - o[2]) + (w[0] * x[1] - w[1] * x[0])
                c = 1.0 / (scale + (r0 * r0 + r1 * r1 + r2 * r2))
                c0, c1, c2 = c * r0, c * r1, c * r2
                y = [c * x[k] for k in range(3)]
                terms = [
                    x[1] * c2 - x[2] * c1,
                    x[2] * c0 - x[0] * c2,
                    x[0] * c1 - x[1] * c0,
                    c0,
                    c1,
                    c2,
                    c,
                    y[0],
                    y[1],
                    y[2],
                    y[0] * x[0],
                    y[1] * x[1],
                    y[2] * x[2],
                    y[0] * x[1],
                    y[0] * x[2],
                    y[1] * x[2],
                ]
                total = terms if total[0] is None else [p + q for p, q in zip(total, terms)]
                terms = [
                    c * m00,
                    c * m11,
                    c * m22,
                    c * m01,
                    c * m02,
                    c * m12,
                    c0 - (w[1] * c2 - w[2] * c1),
                    c1 - (w[2] * c0 - w[0] * c2),
                    c2 - (w[0] * c1 - w[1] * c0),
                ]
                for q, term in enumerate(terms):
                    psum[g, q * 64 + at : q * 64 + at + 8, :] += term
        for q in range(16):
            partial[q * 8 : (q + 1) * 8, :] = total[q]
        return carry

    for g in range(GROUPS):
        lax.fori_loop(g * FOLDED, (g + 1) * FOLDED, functools.partial(step, g), 0)
    finish(PLAIN - 1)
    frame_sums = []
    for q in range(16):
        rows = fsum[pl.ds(q, PLAIN, stride=16), :]
        back = jnp.zeros((FOLDED, 128), jnp.float32)
        for g in range(GROUPS):
            mine = (lane >= g * EXTRA) & (lane < (g + 1) * EXTRA)
            back = jnp.where(mine, pltpu.roll(rows[g * FOLDED : (g + 1) * FOLDED], (g + 1) * EXTRA, 1), back)
        frame_sums += [rows, back]
    frame, position = names_ref[0:1, :], names_ref[1:2, :]
    held = position == row
    own = jnp.where(frame == lax.broadcasted_iota(jnp.int32, (16, 128), 0), scale, 0.0).astype(jnp.bfloat16)
    frames = sum(dot_t(own, piece) for piece in split(jnp.concatenate(frame_sums, axis=0), PARTS))
    for r in range(4):
        pair = frames[:, r * 128 : (r + 1) * 128]
        right[:, 2 * r, :] = half_turn(pair)
        right[:, 2 * r + 1, :] = pair
        sums[:, 10, r, :] = frames[:, (4 + r) * 128 : (5 + r) * 128]
    put_near.wait()
    stores = [pltpu.make_async_copy(sums.at[:, 10], out_hbm.at[:, 10], sems.at[5])]
    stores[0].start()
    own = jnp.where(held, scale, 0.0).astype(jnp.bfloat16)
    for q in range(5):
        wide = 128 if q < 4 else 64
        part = unfold(psum[:, q * 128 : q * 128 + wide, :])
        part = sum(dot_t(own, piece) for piece in split(part, PARTS))
        if wide < 128:
            part = jnp.concatenate([part, jnp.zeros_like(part)], axis=1)
        part = part.reshape(16, 8, 128)
        if wide < 128:
            part = jnp.where(lax.broadcasted_iota(jnp.int32, part.shape, 2) < 64, part, right[...])
        sums[:, 2 * q] = part[:, 0:4]
        sums[:, 2 * q + 1] = part[:, 4:8]
        rows = slice(2 * q, 2 * q + 2)
        stores.append(pltpu.make_async_copy(sums.at[:, rows], out_hbm.at[:, rows], sems.at[q]))
        stores[-1].start()
    wait_all(stores)


def solve3(m00, m11, m22, m01, m02, m12, b0, b1, b2):
    i0 = 1.0 / m00
    l1, l2 = m01 * i0, m02 * i0
    d1 = m11 - l1 * m01
    e = m12 - l1 * m02
    i1 = 1.0 / d1
    l3 = e * i1
    d2 = m22 - l2 * m02 - l3 * e
    y1 = b1 - l1 * b0
    y2 = b2 - l2 * b0 - l3 * y1
    x2 = y2 / d2
    x1 = y1 * i1 - l3 * x2
    x0 = b0 * i0 - l1 * x1 - l2 * x2
    return x0, x1, x2


def new_poses(lower_sums, upper_sums, near_ref, link_ref, edge_ref, first_edge_ref, scratch):
    block, shard = own_frames(), lax.axis_index("tm")
    owners, shards = lax.axis_size("lm"), lax.axis_size("tm")
    lane = lanes((8, 128))
    current, before, after = (half_turn(near_ref[n, :, 128:256]) for n in range(3))
    outside = edge_ref[:, 0:128]
    initial, final = block == 0, block == owners - 1
    before = jnp.where(initial, outside, before)
    after = jnp.where(final, outside, after)
    previous = jnp.where(lane == 0, pltpu.roll(before, 65, 1), pltpu.roll(current, 1, 1))
    following = jnp.where(lane == 63, pltpu.roll(after, 63, 1), pltpu.roll(current, 127, 1))
    motion = link_ref[:, 0:128]
    motion_before = link_ref[:, 128:256]
    outside = pltpu.roll(first_edge_ref[:, 128:256], 65, 1)
    motion_before = jnp.where((lane == 0) & initial, outside, motion_before)
    ends = (lane[0:1] == 63) & final & (shard == shards - 1)
    starts = (lane[0:1] == 0) & initial & (shard == 0)
    weight_after = jnp.where(ends, 0.0, motion[6:7])
    weight_before = jnp.where(starts, 0.0, motion_before[6:7])
    scratch[0:8] = weight_before * (current - previous - motion_before) - weight_after * (
        following - current - motion
    )
    scratch[8:16] = half_turn(lower_sums)
    scratch[16:20] = upper_sums
    scratch[20:24] = half_turn(upper_sums)
    f = [scratch[8 + q : 9 + q, :] for q in range(8)]
    for r in range(4):
        f += [scratch[16 + r : 17 + r, :], scratch[20 + r : 21 + r, :]]
    g = [f[k] + scratch[k : k + 1, :] for k in range(6)]
    diagonal = weight_after + weight_before + damping
    s, c, m = f[6] + diagonal, f[7:10], f[10:16]
    inverse = 1.0 / s
    d = [c[k] * inverse for k in range(3)]
    n00 = m[1] + m[2] + diagonal - (c[1] * d[1] + c[2] * d[2])
    n11 = m[0] + m[2] + diagonal - (c[0] * d[0] + c[2] * d[2])
    n22 = m[0] + m[1] + diagonal - (c[0] * d[0] + c[1] * d[1])
    n01, n02, n12 = c[0] * d[1] - m[3], c[0] * d[2] - m[4], c[1] * d[2] - m[5]
    b0 = g[0] - (d[1] * g[5] - d[2] * g[4])
    b1 = g[1] - (d[2] * g[3] - d[0] * g[5])
    b2 = g[2] - (d[0] * g[4] - d[1] * g[3])
    x0, x1, x2 = solve3(n00, n11, n22, n01, n02, n12, b0, b1, b2)
    x3 = (g[3] + (c[1] * x2 - c[2] * x1)) * inverse
    x4 = (g[4] + (c[2] * x0 - c[0] * x2)) * inverse
    x5 = (g[5] + (c[0] * x1 - c[1] * x0)) * inverse
    for k, x in enumerate((x0, x1, x2, x3, x4, x5)):
        scratch[k : k + 1, :] = x
    return current - scratch[0:8]


def new_points(sums, near_ref):
    x = [near_ref[0, :, 0:128], half_turn(near_ref[0, :, 0:128]), near_ref[0, :, 128:256]]
    q = []
    for pair in sums:
        q += [pair, half_turn(pair)]
    moved = solve3(q[0] + damping, q[1] + damping, q[2] + damping, -q[3], -q[4], -q[5], q[6], q[7], q[8])
    return [x[k] - moved[k] for k in range(3)]


def total(sums_ref, part):
    parts = [sums_ref[d, part] for d in range(sums_ref.shape[0])]
    while len(parts) > 1:
        parts = [p + q for p, q in zip(parts[0::2], parts[1::2])]
    return parts[0]


def pair_total(sums_ref, k):
    return jnp.concatenate([total(sums_ref, 2 * k), total(sums_ref, 2 * k + 1)], axis=0)


def update_kernel(sums_ref, near_hbm, link_hbm, edge_hbm, copies_ref, sent_hbm, *scratch):
    near_ref, link_ref, edge_ref, sent, scratch, sems = scratch
    loads = load_all([near_hbm, link_hbm, edge_hbm], [near_ref, link_ref, edge_ref], sems)
    frames = pair_total(sums_ref, 4), total(sums_ref, 10)
    wait_all(loads)
    lower = lanes((8, 128)) < 64
    pose = new_poses(*frames, near_ref, link_ref, edge_ref, edge_ref, scratch)
    sent[...] = pose
    send = pltpu.make_async_copy(sent, sent_hbm, sems.at[3])
    send.start()
    x = new_points([pair_total(sums_ref, k) for k in range(4)] + [frames[0]], near_ref)
    left = jnp.where(lower, x[0], half_turn(x[1]))
    right = jnp.where(lower, x[2], half_turn(pose))
    for d in range(copies_ref.shape[0]):
        copies_ref[d, :, 0:128] = left
        copies_ref[d, :, 128:256] = right
    send.wait()


def last_poses_kernel(sums_ref, near_hbm, link_hbm, edge_hbm, first_edge_hbm, copies_ref, *scratch):
    near_ref, link_ref, edge_ref, first_edge_ref, scratch, sems = scratch
    sources = [near_hbm, link_hbm, edge_hbm, first_edge_hbm]
    loads = load_all(sources, [near_ref, link_ref, edge_ref, first_edge_ref], sems)
    frames = pair_total(sums_ref, 4), total(sums_ref, 10)
    wait_all(loads)
    pose = new_poses(*frames, near_ref, link_ref, edge_ref, first_edge_ref, scratch)
    lower = lanes((1, 128)) < 64
    for h in range(3):
        pair = jnp.where(lower, pose[2 * h : 2 * h + 1], half_turn(pose[2 * h + 1 : 2 * h + 2]))
        for d in range(copies_ref.shape[0]):
            copies_ref[d, :, h * 128 : (h + 1) * 128] = pair


def last_kernel(copies_ref, sums_ref, near_hbm, poses_ref, points_ref, near_ref, sem):
    load = pltpu.make_async_copy(near_hbm, near_ref, sem)
    load.start()
    owners = copies_ref.shape[0]
    for d in range(owners):
        block = (d + owners // 2 - 1) % owners
        for k in range(6):
            poses_ref[k : k + 1, block * 64 : (block + 1) * 64] = copies_ref[d, :, k * 64 : (k + 1) * 64]
    sums = [pair_total(sums_ref, k) for k in range(5)]
    load.wait()
    x = new_points(sums, near_ref)
    for k in range(3):
        for b in range(8):
            points_ref[k : k + 1, b * 64 : (b + 1) * 64] = x[k][b : b + 1, 0:64]


def call(kernel, outs, scratch, args, spaces, room=48):
    space = {"s": pltpu.SMEM, "v": pltpu.VMEM, "h": pltpu.HBM}
    specs = [pl.BlockSpec(memory_space=space[letter]) for letter in spaces]
    return pl.pallas_call(
        kernel,
        out_shape=outs,
        in_specs=specs[: len(args)],
        out_specs=specs[len(args) :],
        scratch_shapes=scratch,
        compiler_params=pltpu.CompilerParams(vmem_limit_bytes=67_043_328 - (room << 20)),
    )(*args)


def exchange(array):
    return lax.all_to_all(array, "lm", 0, 0, tiled=True)


def on_device(
    camera_poses,
    landmarks,
    odometry,
    odometry_info,
    observations,
    tile_frame,
    tile_block,
    tile_count,
    block_slot,
):
    owners, shards = lax.axis_size("lm"), lax.axis_size("tm")
    slots = observations.shape[0]
    f32 = jnp.float32
    seen = jnp.transpose(observations, (1, 2, 3, 0))
    to_edges = []
    for a in range(shards - 1):
        end, start = a * owners + owners // 2, (a + 1) * owners + owners // 2 + 1
        to_edges += [(end, start), (start, end)]

    def edges(array):
        return lax.ppermute(array, ("tm", "lm"), to_edges)

    def shape(*sizes):
        return jax.ShapeDtypeStruct(sizes, f32)

    def buffer(*sizes):
        return pltpu.VMEM(sizes, f32)

    dma = pltpu.SemaphoreType.DMA
    names = jax.ShapeDtypeStruct((8, 128), jnp.int32)
    copies, sent, link, *names = call(
        pack_kernel,
        [shape(owners, 8, 256), shape(8, 256), shape(8, 256), names, names],
        [
            buffer(*landmarks.shape),
            buffer(*camera_poses.shape),
            buffer(*odometry.shape),
            buffer(1, camera_poses.shape[1]),
            pltpu.VMEM((1, slots), jnp.int32),
            pltpu.VMEM((1, slots), jnp.int32),
            pltpu.VMEM(block_slot.shape, jnp.int32),
            buffer(8, 1024),
            buffer(8, 256),
            buffer(8, 256),
            buffer(8, 256),
            pltpu.VMEM((8, 128), jnp.int32),
            dma((11 + owners,)),
        ],
        [
            tile_count,
            landmarks,
            camera_poses,
            odometry,
            odometry_info[None, :],
            tile_frame[None, :],
            tile_block[None, :],
            block_slot,
        ],
        "shhhhhhhhhhhh",
        0,
    )
    (folded,) = call(
        fold_kernel,
        [jax.ShapeDtypeStruct((3, PLAIN, TILE, 128), seen.dtype)],
        [
            pltpu.VMEM(seen.shape, seen.dtype),
            dma((1 + GROUPS,)),
        ],
        [seen],
        "hv",
        14,
    )
    first_edge = None
    for iteration in range(ITERS):
        window = exchange(copies)
        edge = edges(sent)
        sums, near = call(
            tiles_kernel,
            [shape(owners, 11, 4, 128), shape(3, 8, 256)],
            [
                buffer(3, 8, 256),
                buffer(6 * PLAIN, 128),
                buffer(GROUPS * 192, 128),
                buffer(16 * PLAIN, 128),
                buffer(GROUPS, 576, 128),
                buffer(128, 128),
                buffer(owners, 8, 128),
                buffer(owners, 11, 4, 128),
                dma((8,)),
            ],
            [window, names[iteration], folded],
            "vvvhh",
            14,
        )
        sums = exchange(sums)
        if iteration == 0:
            first_edge = edge
            copies, sent = call(
                update_kernel,
                [shape(owners, 8, 256), shape(8, 128)],
                [buffer(3, 8, 256), buffer(8, 256), buffer(8, 256), buffer(8, 128), buffer(24, 128), dma((4,))],
                [sums, near, link, edge],
                "vhhhvh",
            )
    (copies,) = call(
        last_poses_kernel,
        [shape(owners, 1, 384)],
        [buffer(3, 8, 256), buffer(8, 256), buffer(8, 128), buffer(8, 256), buffer(24, 128), dma((4,))],
        [sums, near, link, edge, first_edge],
        "vhhhhv",
    )
    poses, points = call(
        last_kernel,
        [shape(*camera_poses.shape), shape(*landmarks.shape)],
        [buffer(3, 8, 256), dma],
        [exchange(copies), sums, near],
        "vvhvv",
    )
    return (poses, points)


def solution(mesh):
    return jax.shard_map(
        on_device,
        mesh=mesh,
        in_specs=(
            P(None, "tm"),
            P(None, ("tm", "lm")),
            P(None, "tm"),
            P("tm"),
            P(("tm", "lm"), None, None, None),
            P(("tm", "lm")),
            P(("tm", "lm")),
            P(("tm", "lm")),
            P("tm", None),
        ),
        out_specs=(P(None, "tm"), P(None, ("tm", "lm"))),
        check_vma=False,
    )
```

```python
import functools

import jax
import jax.numpy as jnp
from jax import lax
from jax.experimental import pallas as pl
from jax.experimental.pallas import tpu as pltpu
from jax.sharding import PartitionSpec as P

TILE = 64
ITERS = 2
SLOTS = 96
EXTRA = 128 - SLOTS
GROUPS = SLOTS // EXTRA
PLAIN = TILE * SLOTS // 128
FOLDED = TILE - PLAIN
PARTS = 2
damping = 1.0
scale = 4.0


def lanes(shape):
    return lax.broadcasted_iota(jnp.int32, shape, 1)


def half_turn(x):
    return pltpu.roll(x, 64, 1)


def own_frames():
    owners = lax.axis_size("lm")
    return lax.rem(lax.axis_index("lm") + owners // 2 - 1, owners)


def own_block(ref, block):
    pair = jnp.zeros((8, 128), jnp.float32)
    for h in range(8):
        pair = jnp.where(block // 2 == h, ref[:, h * 128 : (h + 1) * 128], pair)
    return jnp.where(block % 2 == 1, half_turn(pair), pair)


def load_all(sources, targets, sems):
    loads = [pltpu.make_async_copy(a, b, sems.at[n]) for n, (a, b) in enumerate(zip(sources, targets))]
    for load in loads:
        load.start()
    return loads


def wait_all(loads):
    for load in loads:
        load.wait()


def pack_kernel(
    count_ref,
    points_hbm,
    poses_hbm,
    odometry_hbm,
    info_hbm,
    frame_hbm,
    block_hbm,
    slot_hbm,
    copies_hbm,
    edge_hbm,
    link_hbm,
    names_hbm,
    more_names_hbm,
    points,
    poses,
    odometry,
    info,
    frame,
    block,
    slot,
    rows,
    chunk,
    edge,
    link_ref,
    names_ref,
    sems,
):
    loads = [
        pltpu.make_async_copy(source, target, sems.at[n])
        for n, (source, target) in enumerate(
            [
                (poses_hbm, poses),
                (points_hbm, points),
                (odometry_hbm, odometry),
                (info_hbm, info),
                (frame_hbm, frame),
                (block_hbm, block),
                (slot_hbm, slot),
            ]
        )
    ]
    for load in loads:
        load.start()
    rows[...] = jnp.zeros((8, 1024), jnp.float32)
    block_of_frames = own_frames()
    lane = lanes((8, 128))
    for load in loads:
        load.wait()
    rows[0:6, :] = poses[...]
    pose = own_block(rows, block_of_frames)
    for k in range(3):
        for b in range(8):
            chunk[b : b + 1, k * 64 : (k + 1) * 64] = points[k : k + 1, b * 64 : (b + 1) * 64]
    chunk[:, 192:256] = half_turn(pose)[:, 64:128]
    owners = copies_hbm.shape[0]
    sends = [pltpu.make_async_copy(chunk, copies_hbm.at[d], sems.at[10 + d]) for d in range(owners)]
    for send in sends:
        send.start()
    rows[0:6, :] = odometry[...]
    rows[6:7, :] = info[...]
    current = own_block(rows, block_of_frames)
    before = own_block(rows, block_of_frames - 1)
    edge[:, 0:128] = pose
    edge[:, 128:256] = current
    sends.append(pltpu.make_async_copy(edge, edge_hbm, sems.at[7]))
    sends[-1].start()
    link_ref[:, 0:128] = current
    link_ref[:, 128:256] = jnp.where(lane == 0, pltpu.roll(before, 65, 1), pltpu.roll(current, 1, 1))
    sends.append(pltpu.make_async_copy(link_ref, link_hbm, sems.at[8]))
    sends[-1].start()
    slots = frame.shape[1]
    row = lax.broadcasted_iota(jnp.int32, (128, slots), 0)
    named = jnp.where(block[...] == row, 1.0, 0.0).astype(jnp.bfloat16)
    table = jnp.broadcast_to(slot[...].astype(jnp.float32), (8, 128)).astype(jnp.bfloat16)
    position = dot(table, named)[0:1].astype(jnp.int32)
    live = lanes((1, slots)) < count_ref[0]
    names_ref[...] = jnp.full(names_ref.shape, -1, jnp.int32)
    names_ref[0:1, 0:slots] = jnp.where(live, (frame[...] + owners // 2 + 1) & (owners - 1), -1)
    names_ref[1:2, 0:slots] = jnp.where(live, position, -1)
    for n in range(2):
        name = names_ref[...][n : n + 1]
        for g in range(GROUPS):
            folded = jnp.where(lane[0:1] < SLOTS, name, pltpu.roll(name, SLOTS - g * EXTRA, 1))
            names_ref[2 + n * GROUPS + g : 3 + n * GROUPS + g, :] = folded
    sends.append(pltpu.make_async_copy(names_ref, names_hbm, sems.at[9]))
    sends[-1].start()
    sends.append(pltpu.make_async_copy(names_ref, more_names_hbm, sems.at[10 + owners]))
    sends[-1].start()
    for send in sends:
        send.wait()


def split(x, parts):
    pieces = []
    for _ in range(parts - 1):
        pieces.append(x.astype(jnp.bfloat16))
        x = x - pieces[-1].astype(jnp.float32)
    pieces.append(x.astype(jnp.bfloat16))
    return pieces


def dot(a, b):
    return lax.dot_general(a, b, (((1,), (0,)), ((), ())), preferred_element_type=jnp.float32)


def dot_t(a, b):
    return lax.dot_general(a, b, (((1,), (1,)), ((), ())), preferred_element_type=jnp.float32)


def fold_kernel(seen_hbm, folded, seen, sems):
    parts = [pl.ds(PLAIN, FOLDED)] + [pl.ds(g * FOLDED, FOLDED) for g in range(GROUPS)]
    loads = [
        pltpu.make_async_copy(seen_hbm.at[k, part], seen.at[k, part], sems.at[n, k])
        for n, part in enumerate(parts)
        for k in range(3)
    ]
    for load in loads:
        load.start()
    for g in range(GROUPS):
        for k in range(3):
            if g == 0:
                loads[k].wait()
            loads[3 + g * 3 + k].wait()

            def step(m, carry):
                for r in range(0, TILE, 16):
                    wide = seen[k, g * FOLDED + m, r : r + 16, :]
                    more = seen[k, PLAIN + m, r : r + 16, g * EXTRA : (g + 1) * EXTRA]
                    folded[k, g * FOLDED + m, r : r + 16, :] = jnp.concatenate([wide, more], axis=1)
                return carry

            lax.fori_loop(0, FOLDED, step, 0, unroll=4)


def unfold(parts):
    lane = lanes(parts.shape[1:])
    result = jnp.where(lane < SLOTS, sum(parts[g] for g in range(GROUPS)), 0.0)
    for g in range(GROUPS):
        mine = (lane >= g * EXTRA) & (lane < (g + 1) * EXTRA)
        result = result + jnp.where(mine, pltpu.roll(parts[g], (g + 1) * EXTRA, 1), 0.0)
    return result


def pick_poses(turned, names_ref, pose):
    row = lax.broadcasted_iota(jnp.int32, (128, 128), 0)
    lane = lanes((FOLDED, 128))
    for g in range(GROUPS):
        frame = names_ref[2 + g : 3 + g, :]
        at = g * FOLDED
        poses = jnp.concatenate([piece[r : r + FOLDED] for r in (at, PLAIN) for piece in turned], axis=0)
        for k in range(6):
            pick = jnp.where(frame * 8 + k == row, 1.0, 0.0).astype(jnp.bfloat16)
            both = dot(poses, pick)
            found = [both[n * FOLDED : (n + 1) * FOLDED] for n in range(2 * PARTS)]
            found = [sum(found[:PARTS]), sum(found[PARTS:])]
            pose[k * PLAIN + at : k * PLAIN + at + FOLDED, :] = jnp.where(lane < SLOTS, *found)


def tiles_kernel(window_ref, names_ref, seen_ref, out_hbm, near_hbm, near_ref, pose, sem, *scratch):
    owner, owners = lax.axis_index("lm"), lax.axis_size("lm")
    near_ref[0] = window_ref[owner]
    near_ref[1] = window_ref[lax.rem(owner + owners - 1, owners)]
    near_ref[2] = window_ref[lax.rem(owner + 1, owners)]
    put_near = pltpu.make_async_copy(near_ref, near_hbm, sem)
    put_near.start()
    turned = split(jnp.transpose(window_ref[...].reshape(128, 256), (1, 0)), PARTS)
    pick_poses([piece[192:256] for piece in turned], names_ref, pose)
    points = [piece[0:192] for piece in turned]
    add_tiles(points, names_ref, seen_ref, pose, out_hbm, *scratch)
    put_near.wait()


def add_tiles(points, names_ref, seen_ref, pose, out_hbm, point, fsum, psum, partial, right, sums, sems):
    row = lax.broadcasted_iota(jnp.int32, (128, 128), 0)
    lane = lanes((FOLDED, 128))
    points = jnp.concatenate(points, axis=0)
    for g in range(GROUPS):
        position = names_ref[2 + GROUPS + g : 3 + GROUPS + g, :]
        pick = jnp.where(position == row, 1.0, 0.0).astype(jnp.bfloat16)
        found = dot(points, pick)
        point[g * 192 : (g + 1) * 192, :] = sum(found[n * 192 : (n + 1) * 192] for n in range(PARTS))
    psum[...] = jnp.zeros_like(psum)
    partial[...] = jnp.zeros_like(partial)

    sub = lax.broadcasted_iota(jnp.int32, (8, 128), 0)

    def merge(a, b, shift):
        low = (sub // shift) % 2 == 0
        if shift == 4:
            return jnp.where(low, a, b) + pltpu.roll(jnp.where(low, b, a), 4, 0)
        return jnp.where(low, a + pltpu.roll(a, 8 - shift, 0), b + pltpu.roll(b, shift, 0))

    def finish(i):
        for half in range(2):
            parts = [partial[(half * 8 + q) * 8 : (half * 8 + q + 1) * 8, :] for q in range(8)]
            for shift in (4, 2, 1):
                count = len(parts) // 2
                parts = [merge(parts[q], parts[q + count], shift) for q in range(count)]
            fsum[pl.ds(pl.multiple_of(i * 16 + half * 8, 8), 8), :] = parts[0]

    def step(g, i, carry):
        finish(jnp.maximum(i - 1, 0))
        w = [jnp.broadcast_to(pose[pl.ds(k * PLAIN + i, 1), :], (8, 128)) for k in range(3)]
        t = [jnp.broadcast_to(pose[pl.ds((3 + k) * PLAIN + i, 1), :], (8, 128)) for k in range(3)]
        w00, w11, w22 = w[0] * w[0], w[1] * w[1], w[2] * w[2]
        m00, m11, m22 = 1.0 + (w11 + w22), 1.0 + (w00 + w22), 1.0 + (w00 + w11)
        m01, m02, m12 = w[0] * w[1], w[0] * w[2], w[1] * w[2]
        total = [None] * 16
        for part in range(0, TILE, 16):
            seen = [seen_ref[k, i, part : part + 16, :].astype(jnp.float32) for k in range(3)]
            for h in range(2):
                at = part + h * 8
                x = [point[(g * 3 + k) * 64 + at : (g * 3 + k) * 64 + at + 8, :] for k in range(3)]
                o = [seen[k][h * 8 : (h + 1) * 8] for k in range(3)]
                r0 = (x[0] + t[0] - o[0]) + (w[1] * x[2] - w[2] * x[1])
                r1 = (x[1] + t[1] - o[1]) + (w[2] * x[0] - w[0] * x[2])
                r2 = (x[2] + t[2] - o[2]) + (w[0] * x[1] - w[1] * x[0])
                c = 1.0 / (scale + (r0 * r0 + r1 * r1 + r2 * r2))
                c0, c1, c2 = c * r0, c * r1, c * r2
                y = [c * x[k] for k in range(3)]
                terms = [
                    x[1] * c2 - x[2] * c1,
                    x[2] * c0 - x[0] * c2,
                    x[0] * c1 - x[1] * c0,
                    c0,
                    c1,
                    c2,
                    c,
                    y[0],
                    y[1],
                    y[2],
                    y[0] * x[0],
                    y[1] * x[1],
                    y[2] * x[2],
                    y[0] * x[1],
                    y[0] * x[2],
                    y[1] * x[2],
                ]
                total = terms if total[0] is None else [p + q for p, q in zip(total, terms)]
                terms = [
                    c * m00,
                    c * m11,
                    c * m22,
                    c * m01,
                    c * m02,
                    c * m12,
                    c0 - (w[1] * c2 - w[2] * c1),
                    c1 - (w[2] * c0 - w[0] * c2),
                    c2 - (w[0] * c1 - w[1] * c0),
                ]
                for q, term in enumerate(terms):
                    psum[g, q * 64 + at : q * 64 + at + 8, :] += term
        for q in range(16):
            partial[q * 8 : (q + 1) * 8, :] = total[q]
        return carry

    for g in range(GROUPS):
        lax.fori_loop(g * FOLDED, (g + 1) * FOLDED, functools.partial(step, g), 0)
    finish(PLAIN - 1)
    frame_sums = []
    for q in range(16):
        rows = fsum[pl.ds(q, PLAIN, stride=16), :]
        back = jnp.zeros((FOLDED, 128), jnp.float32)
        for g in range(GROUPS):
            mine = (lane >= g * EXTRA) & (lane < (g + 1) * EXTRA)
            back = jnp.where(mine, pltpu.roll(rows[g * FOLDED : (g + 1) * FOLDED], (g + 1) * EXTRA, 1), back)
        frame_sums += [rows, back]
    frame, position = names_ref[0:1, :], names_ref[1:2, :]
    held = position == row
    own = jnp.where(frame == lax.broadcasted_iota(jnp.int32, (16, 128), 0), scale, 0.0).astype(jnp.bfloat16)
    frames = sum(dot_t(own, piece) for piece in split(jnp.concatenate(frame_sums, axis=0), PARTS))
    for r in range(4):
        pair = frames[:, r * 128 : (r + 1) * 128]
        right[:, 2 * r, :] = half_turn(pair)
        right[:, 2 * r + 1, :] = pair
        sums[:, 10, r, :] = frames[:, (4 + r) * 128 : (5 + r) * 128]
    stores = [pltpu.make_async_copy(sums.at[:, 10], out_hbm.at[:, 10], sems.at[5])]
    stores[0].start()
    own = jnp.where(held, scale, 0.0).astype(jnp.bfloat16)
    for q in range(5):
        wide = 128 if q < 4 else 64
        part = unfold(psum[:, q * 128 : q * 128 + wide, :])
        part = sum(dot_t(own, piece) for piece in split(part, PARTS))
        if wide < 128:
            part = jnp.concatenate([part, jnp.zeros_like(part)], axis=1)
        part = part.reshape(16, 8, 128)
        if wide < 128:
            part = jnp.where(lax.broadcasted_iota(jnp.int32, part.shape, 2) < 64, part, right[...])
        sums[:, 2 * q] = part[:, 0:4]
        sums[:, 2 * q + 1] = part[:, 4:8]
        rows = slice(2 * q, 2 * q + 2)
        stores.append(pltpu.make_async_copy(sums.at[:, rows], out_hbm.at[:, rows], sems.at[q]))
        stores[-1].start()
    wait_all(stores)


def solve3(m00, m11, m22, m01, m02, m12, b0, b1, b2):
    i0 = 1.0 / m00
    l1, l2 = m01 * i0, m02 * i0
    d1 = m11 - l1 * m01
    e = m12 - l1 * m02
    i1 = 1.0 / d1
    l3 = e * i1
    d2 = m22 - l2 * m02 - l3 * e
    y1 = b1 - l1 * b0
    y2 = b2 - l2 * b0 - l3 * y1
    x2 = y2 / d2
    x1 = y1 * i1 - l3 * x2
    x0 = b0 * i0 - l1 * x1 - l2 * x2
    return x0, x1, x2


def new_poses(lower_sums, upper_sums, near_ref, link_ref, edge_ref, first_edge_ref, scratch):
    block, shard = own_frames(), lax.axis_index("tm")
    owners, shards = lax.axis_size("lm"), lax.axis_size("tm")
    lane = lanes((8, 128))
    current, before, after = (half_turn(near_ref[n, :, 128:256]) for n in range(3))
    outside = edge_ref[:, 0:128]
    initial, final = block == 0, block == owners - 1
    before = jnp.where(initial, outside, before)
    after = jnp.where(final, outside, after)
    previous = jnp.where(lane == 0, pltpu.roll(before, 65, 1), pltpu.roll(current, 1, 1))
    following = jnp.where(lane == 63, pltpu.roll(after, 63, 1), pltpu.roll(current, 127, 1))
    motion = link_ref[:, 0:128]
    motion_before = link_ref[:, 128:256]
    outside = pltpu.roll(first_edge_ref[:, 128:256], 65, 1)
    motion_before = jnp.where((lane == 0) & initial, outside, motion_before)
    ends = (lane[0:1] == 63) & final & (shard == shards - 1)
    starts = (lane[0:1] == 0) & initial & (shard == 0)
    weight_after = jnp.where(ends, 0.0, motion[6:7])
    weight_before = jnp.where(starts, 0.0, motion_before[6:7])
    scratch[0:8] = weight_before * (current - previous - motion_before) - weight_after * (
        following - current - motion
    )
    scratch[8:16] = half_turn(lower_sums)
    scratch[16:20] = upper_sums
    scratch[20:24] = half_turn(upper_sums)
    f = [scratch[8 + q : 9 + q, :] for q in range(8)]
    for r in range(4):
        f += [scratch[16 + r : 17 + r, :], scratch[20 + r : 21 + r, :]]
    g = [f[k] + scratch[k : k + 1, :] for k in range(6)]
    diagonal = weight_after + weight_before + damping
    s, c, m = f[6] + diagonal, f[7:10], f[10:16]
    inverse = 1.0 / s
    d = [c[k] * inverse for k in range(3)]
    n00 = m[1] + m[2] + diagonal - (c[1] * d[1] + c[2] * d[2])
    n11 = m[0] + m[2] + diagonal - (c[0] * d[0] + c[2] * d[2])
    n22 = m[0] + m[1] + diagonal - (c[0] * d[0] + c[1] * d[1])
    n01, n02, n12 = c[0] * d[1] - m[3], c[0] * d[2] - m[4], c[1] * d[2] - m[5]
    b0 = g[0] - (d[1] * g[5] - d[2] * g[4])
    b1 = g[1] - (d[2] * g[3] - d[0] * g[5])
    b2 = g[2] - (d[0] * g[4] - d[1] * g[3])
    x0, x1, x2 = solve3(n00, n11, n22, n01, n02, n12, b0, b1, b2)
    x3 = (g[3] + (c[1] * x2 - c[2] * x1)) * inverse
    x4 = (g[4] + (c[2] * x0 - c[0] * x2)) * inverse
    x5 = (g[5] + (c[0] * x1 - c[1] * x0)) * inverse
    for k, x in enumerate((x0, x1, x2, x3, x4, x5)):
        scratch[k : k + 1, :] = x
    return current - scratch[0:8]


def new_points(sums, near_ref):
    x = [near_ref[0, :, 0:128], half_turn(near_ref[0, :, 0:128]), near_ref[0, :, 128:256]]
    q = []
    for pair in sums:
        q += [pair, half_turn(pair)]
    moved = solve3(q[0] + damping, q[1] + damping, q[2] + damping, -q[3], -q[4], -q[5], q[6], q[7], q[8])
    return [x[k] - moved[k] for k in range(3)]


def total(sums_ref, part):
    parts = [sums_ref[d, part] for d in range(sums_ref.shape[0])]
    while len(parts) > 1:
        parts = [p + q for p, q in zip(parts[0::2], parts[1::2])]
    return parts[0]


def pair_total(sums_ref, k):
    return jnp.concatenate([total(sums_ref, 2 * k), total(sums_ref, 2 * k + 1)], axis=0)


def update_kernel(sums_ref, near_hbm, link_hbm, edge_hbm, copies_ref, sent_hbm, *scratch):
    near_ref, link_ref, edge_ref, sent, scratch, sems = scratch
    loads = load_all([near_hbm, link_hbm, edge_hbm], [near_ref, link_ref, edge_ref], sems)
    frames = pair_total(sums_ref, 4), total(sums_ref, 10)
    wait_all(loads)
    lower = lanes((8, 128)) < 64
    pose = new_poses(*frames, near_ref, link_ref, edge_ref, edge_ref, scratch)
    sent[...] = pose
    send = pltpu.make_async_copy(sent, sent_hbm, sems.at[3])
    send.start()
    x = new_points([pair_total(sums_ref, k) for k in range(4)] + [frames[0]], near_ref)
    left = jnp.where(lower, x[0], half_turn(x[1]))
    right = jnp.where(lower, x[2], half_turn(pose))
    for d in range(copies_ref.shape[0]):
        copies_ref[d, :, 0:128] = left
        copies_ref[d, :, 128:256] = right
    send.wait()


def last_poses_kernel(sums_ref, near_hbm, link_hbm, edge_hbm, first_edge_hbm, copies_ref, *scratch):
    near_ref, link_ref, edge_ref, first_edge_ref, scratch, sems = scratch
    sources = [near_hbm, link_hbm, edge_hbm, first_edge_hbm]
    loads = load_all(sources, [near_ref, link_ref, edge_ref, first_edge_ref], sems)
    frames = pair_total(sums_ref, 4), total(sums_ref, 10)
    wait_all(loads)
    pose = new_poses(*frames, near_ref, link_ref, edge_ref, first_edge_ref, scratch)
    lower = lanes((1, 128)) < 64
    for h in range(3):
        pair = jnp.where(lower, pose[2 * h : 2 * h + 1], half_turn(pose[2 * h + 1 : 2 * h + 2]))
        for d in range(copies_ref.shape[0]):
            copies_ref[d, :, h * 128 : (h + 1) * 128] = pair


def last_kernel(copies_ref, sums_ref, near_hbm, poses_ref, points_ref, near_ref, sem):
    load = pltpu.make_async_copy(near_hbm, near_ref, sem)
    load.start()
    owners = copies_ref.shape[0]
    for d in range(owners):
        block = (d + owners // 2 - 1) % owners
        for k in range(6):
            poses_ref[k : k + 1, block * 64 : (block + 1) * 64] = copies_ref[d, :, k * 64 : (k + 1) * 64]
    sums = [pair_total(sums_ref, k) for k in range(5)]
    load.wait()
    x = new_points(sums, near_ref)
    for k in range(3):
        for b in range(8):
            points_ref[k : k + 1, b * 64 : (b + 1) * 64] = x[k][b : b + 1, 0:64]


def call(kernel, outs, scratch, args, spaces, room=48):
    space = {"s": pltpu.SMEM, "v": pltpu.VMEM, "h": pltpu.HBM}
    specs = [pl.BlockSpec(memory_space=space[letter]) for letter in spaces]
    return pl.pallas_call(
        kernel,
        out_shape=outs,
        in_specs=specs[: len(args)],
        out_specs=specs[len(args) :],
        scratch_shapes=scratch,
        compiler_params=pltpu.CompilerParams(vmem_limit_bytes=67_043_328 - (room << 20)),
    )(*args)


def exchange(array):
    return lax.all_to_all(array, "lm", 0, 0, tiled=True)


def on_device(
    camera_poses,
    landmarks,
    odometry,
    odometry_info,
    observations,
    tile_frame,
    tile_block,
    tile_count,
    block_slot,
):
    owners, shards = lax.axis_size("lm"), lax.axis_size("tm")
    slots = observations.shape[0]
    f32 = jnp.float32
    seen = jnp.transpose(observations, (1, 2, 3, 0))
    to_edges = []
    for a in range(shards - 1):
        end, start = a * owners + owners // 2, (a + 1) * owners + owners // 2 + 1
        to_edges += [(end, start), (start, end)]

    def edges(array):
        return lax.ppermute(array, ("tm", "lm"), to_edges)

    def shape(*sizes):
        return jax.ShapeDtypeStruct(sizes, f32)

    def buffer(*sizes):
        return pltpu.VMEM(sizes, f32)

    dma = pltpu.SemaphoreType.DMA
    names = jax.ShapeDtypeStruct((8, 128), jnp.int32)
    copies, sent, link, *names = call(
        pack_kernel,
        [shape(owners, 8, 256), shape(8, 256), shape(8, 256), names, names],
        [
            buffer(*landmarks.shape),
            buffer(*camera_poses.shape),
            buffer(*odometry.shape),
            buffer(1, camera_poses.shape[1]),
            pltpu.VMEM((1, slots), jnp.int32),
            pltpu.VMEM((1, slots), jnp.int32),
            pltpu.VMEM(block_slot.shape, jnp.int32),
            buffer(8, 1024),
            buffer(8, 256),
            buffer(8, 256),
            buffer(8, 256),
            pltpu.VMEM((8, 128), jnp.int32),
            dma((11 + owners,)),
        ],
        [
            tile_count,
            landmarks,
            camera_poses,
            odometry,
            odometry_info[None, :],
            tile_frame[None, :],
            tile_block[None, :],
            block_slot,
        ],
        "shhhhhhhhhhhh",
        0,
    )
    (folded,) = call(
        fold_kernel,
        [jax.ShapeDtypeStruct((3, PLAIN, TILE, 128), seen.dtype)],
        [
            pltpu.VMEM(seen.shape, seen.dtype),
            dma((1 + GROUPS, 3)),
        ],
        [seen],
        "hv",
        14,
    )
    first_edge = None
    for iteration in range(ITERS):
        window = exchange(copies)
        edge = edges(sent)
        sums, near = call(
            tiles_kernel,
            [shape(owners, 11, 4, 128), shape(3, 8, 256)],
            [
                buffer(3, 8, 256),
                buffer(6 * PLAIN, 128),
                dma,
                buffer(GROUPS * 192, 128),
                buffer(16 * PLAIN, 128),
                buffer(GROUPS, 576, 128),
                buffer(128, 128),
                buffer(owners, 8, 128),
                buffer(owners, 11, 4, 128),
                dma((6,)),
            ],
            [window, names[iteration], folded],
            "vvvhh",
            14,
        )
        sums = exchange(sums)
        if iteration == 0:
            first_edge = edge
            copies, sent = call(
                update_kernel,
                [shape(owners, 8, 256), shape(8, 128)],
                [buffer(3, 8, 256), buffer(8, 256), buffer(8, 256), buffer(8, 128), buffer(24, 128), dma((4,))],
                [sums, near, link, edge],
                "vhhhvh",
            )
    (copies,) = call(
        last_poses_kernel,
        [shape(owners, 1, 384)],
        [buffer(3, 8, 256), buffer(8, 256), buffer(8, 128), buffer(8, 256), buffer(24, 128), dma((4,))],
        [sums, near, link, edge, first_edge],
        "vhhhhv",
    )
    poses, points = call(
        last_kernel,
        [shape(*camera_poses.shape), shape(*landmarks.shape)],
        [buffer(3, 8, 256), dma],
        [exchange(copies), sums, near],
        "vvhvv",
    )
    return (poses, points)


def solution(mesh):
    return jax.shard_map(
        on_device,
        mesh=mesh,
        in_specs=(
            P(None, "tm"),
            P(None, ("tm", "lm")),
            P(None, "tm"),
            P("tm"),
            P(("tm", "lm"), None, None, None),
            P(("tm", "lm")),
            P(("tm", "lm")),
            P(("tm", "lm")),
            P("tm", None),
        ),
        out_specs=(P(None, "tm"), P(None, ("tm", "lm"))),
        check_vma=False,
    )
```

```python
import functools

import jax
import jax.numpy as jnp
from jax import lax
from jax.experimental import pallas as pl
from jax.experimental.pallas import tpu as pltpu
from jax.sharding import PartitionSpec as P

TILE = 64
ITERS = 2
SLOTS = 96
EXTRA = 128 - SLOTS
GROUPS = SLOTS // EXTRA
PLAIN = TILE * SLOTS // 128
FOLDED = TILE - PLAIN
PARTS = 2
damping = 1.0
scale = 4.0


def lanes(shape):
    return lax.broadcasted_iota(jnp.int32, shape, 1)


def half_turn(x):
    return pltpu.roll(x, 64, 1)


def own_frames():
    owners = lax.axis_size("lm")
    return lax.rem(lax.axis_index("lm") + owners // 2 - 1, owners)


def own_block(ref, block):
    pair = jnp.zeros((8, 128), jnp.float32)
    for h in range(8):
        pair = jnp.where(block // 2 == h, ref[:, h * 128 : (h + 1) * 128], pair)
    return jnp.where(block % 2 == 1, half_turn(pair), pair)


def load_all(sources, targets, sems):
    loads = [pltpu.make_async_copy(a, b, sems.at[n]) for n, (a, b) in enumerate(zip(sources, targets))]
    for load in loads:
        load.start()
    return loads


def wait_all(loads):
    for load in loads:
        load.wait()


def pack_kernel(
    count_ref,
    points_hbm,
    poses_hbm,
    odometry_hbm,
    info_hbm,
    frame_hbm,
    block_hbm,
    slot_hbm,
    copies_hbm,
    edge_hbm,
    link_hbm,
    names_hbm,
    more_names_hbm,
    points,
    poses,
    odometry,
    info,
    frame,
    block,
    slot,
    rows,
    chunk,
    edge,
    link_ref,
    names_ref,
    sems,
):
    loads = [
        pltpu.make_async_copy(source, target, sems.at[n])
        for n, (source, target) in enumerate(
            [
                (poses_hbm, poses),
                (points_hbm, points),
                (odometry_hbm, odometry),
                (info_hbm, info),
                (frame_hbm, frame),
                (block_hbm, block),
                (slot_hbm, slot),
            ]
        )
    ]
    for load in loads:
        load.start()
    rows[...] = jnp.zeros((8, 1024), jnp.float32)
    block_of_frames = own_frames()
    lane = lanes((8, 128))
    wait_all(loads[:2])
    rows[0:6, :] = poses[...]
    pose = own_block(rows, block_of_frames)
    for k in range(3):
        for b in range(8):
            chunk[b : b + 1, k * 64 : (k + 1) * 64] = points[k : k + 1, b * 64 : (b + 1) * 64]
    chunk[:, 192:256] = half_turn(pose)[:, 64:128]
    owners = copies_hbm.shape[0]
    sends = [pltpu.make_async_copy(chunk, copies_hbm.at[d], sems.at[10 + d]) for d in range(owners)]
    for send in sends:
        send.start()
    wait_all(loads[2:])
    rows[0:6, :] = odometry[...]
    rows[6:7, :] = info[...]
    current = own_block(rows, block_of_frames)
    before = own_block(rows, block_of_frames - 1)
    edge[:, 0:128] = pose
    edge[:, 128:256] = current
    sends.append(pltpu.make_async_copy(edge, edge_hbm, sems.at[7]))
    sends[-1].start()
    link_ref[:, 0:128] = current
    link_ref[:, 128:256] = jnp.where(lane == 0, pltpu.roll(before, 65, 1), pltpu.roll(current, 1, 1))
    sends.append(pltpu.make_async_copy(link_ref, link_hbm, sems.at[8]))
    sends[-1].start()
    slots = frame.shape[1]
    row = lax.broadcasted_iota(jnp.int32, (128, slots), 0)
    named = jnp.where(block[...] == row, 1.0, 0.0).astype(jnp.bfloat16)
    table = jnp.broadcast_to(slot[...].astype(jnp.float32), (8, 128)).astype(jnp.bfloat16)
    position = dot(table, named)[0:1].astype(jnp.int32)
    live = lanes((1, slots)) < count_ref[0]
    names_ref[...] = jnp.full(names_ref.shape, -1, jnp.int32)
    names_ref[0:1, 0:slots] = jnp.where(live, (frame[...] + owners // 2 + 1) & (owners - 1), -1)
    names_ref[1:2, 0:slots] = jnp.where(live, position, -1)
    for n in range(2):
        name = names_ref[...][n : n + 1]
        for g in range(GROUPS):
            folded = jnp.where(lane[0:1] < SLOTS, name, pltpu.roll(name, SLOTS - g * EXTRA, 1))
            names_ref[2 + n * GROUPS + g : 3 + n * GROUPS + g, :] = folded
    sends.append(pltpu.make_async_copy(names_ref, names_hbm, sems.at[9]))
    sends[-1].start()
    sends.append(pltpu.make_async_copy(names_ref, more_names_hbm, sems.at[10 + owners]))
    sends[-1].start()
    for send in sends:
        send.wait()


def split(x, parts):
    pieces = []
    for _ in range(parts - 1):
        pieces.append(x.astype(jnp.bfloat16))
        x = x - pieces[-1].astype(jnp.float32)
    pieces.append(x.astype(jnp.bfloat16))
    return pieces


def dot(a, b):
    return lax.dot_general(a, b, (((1,), (0,)), ((), ())), preferred_element_type=jnp.float32)


def dot_t(a, b):
    return lax.dot_general(a, b, (((1,), (1,)), ((), ())), preferred_element_type=jnp.float32)


def fold_kernel(seen_hbm, folded, seen, sems):
    parts = [pl.ds(PLAIN, FOLDED)] + [pl.ds(g * FOLDED, FOLDED) for g in range(GROUPS)]
    loads = [
        pltpu.make_async_copy(seen_hbm.at[k, part], seen.at[k, part], sems.at[n, k])
        for n, part in enumerate(parts)
        for k in range(3)
    ]
    for load in loads:
        load.start()
    for g in range(GROUPS):
        for k in range(3):
            if g == 0:
                loads[k].wait()
            loads[3 + g * 3 + k].wait()

            def step(m, carry):
                for r in range(0, TILE, 16):
                    wide = seen[k, g * FOLDED + m, r : r + 16, :]
                    more = seen[k, PLAIN + m, r : r + 16, g * EXTRA : (g + 1) * EXTRA]
                    folded[k, g * FOLDED + m, r : r + 16, :] = jnp.concatenate([wide, more], axis=1)
                return carry

            lax.fori_loop(0, FOLDED, step, 0, unroll=4)


def unfold(parts):
    lane = lanes(parts.shape[1:])
    result = jnp.where(lane < SLOTS, sum(parts[g] for g in range(GROUPS)), 0.0)
    for g in range(GROUPS):
        mine = (lane >= g * EXTRA) & (lane < (g + 1) * EXTRA)
        result = result + jnp.where(mine, pltpu.roll(parts[g], (g + 1) * EXTRA, 1), 0.0)
    return result


def pick_poses(turned, names_ref, pose):
    row = lax.broadcasted_iota(jnp.int32, (128, 128), 0)
    lane = lanes((FOLDED, 128))
    for g in range(GROUPS):
        frame = names_ref[2 + g : 3 + g, :]
        at = g * FOLDED
        poses = jnp.concatenate([piece[r : r + FOLDED] for r in (at, PLAIN) for piece in turned], axis=0)
        for k in range(6):
            pick = jnp.where(frame * 8 + k == row, 1.0, 0.0).astype(jnp.bfloat16)
            both = dot(poses, pick)
            found = [both[n * FOLDED : (n + 1) * FOLDED] for n in range(2 * PARTS)]
            found = [sum(found[:PARTS]), sum(found[PARTS:])]
            pose[k * PLAIN + at : k * PLAIN + at + FOLDED, :] = jnp.where(lane < SLOTS, *found)


def tiles_kernel(window_ref, names_ref, seen_ref, out_hbm, near_hbm, near_ref, pose, sem, *scratch):
    owner, owners = lax.axis_index("lm"), lax.axis_size("lm")
    near_ref[0] = window_ref[owner]
    near_ref[1] = window_ref[lax.rem(owner + owners - 1, owners)]
    near_ref[2] = window_ref[lax.rem(owner + 1, owners)]
    put_near = pltpu.make_async_copy(near_ref, near_hbm, sem)
    put_near.start()
    turned = split(jnp.transpose(window_ref[...].reshape(128, 256), (1, 0)), PARTS)
    pick_poses([piece[192:256] for piece in turned], names_ref, pose)
    points = [piece[0:192] for piece in turned]
    add_tiles(points, names_ref, seen_ref, pose, out_hbm, *scratch)
    put_near.wait()


def add_tiles(points, names_ref, seen_ref, pose, out_hbm, point, fsum, psum, partial, right, sums, sems):
    row = lax.broadcasted_iota(jnp.int32, (128, 128), 0)
    lane = lanes((FOLDED, 128))
    points = jnp.concatenate(points, axis=0)
    for g in range(GROUPS):
        position = names_ref[2 + GROUPS + g : 3 + GROUPS + g, :]
        pick = jnp.where(position == row, 1.0, 0.0).astype(jnp.bfloat16)
        found = dot(points, pick)
        point[g * 192 : (g + 1) * 192, :] = sum(found[n * 192 : (n + 1) * 192] for n in range(PARTS))
    psum[...] = jnp.zeros_like(psum)
    partial[...] = jnp.zeros_like(partial)

    sub = lax.broadcasted_iota(jnp.int32, (8, 128), 0)

    def merge(a, b, shift):
        low = (sub // shift) % 2 == 0
        if shift == 4:
            return jnp.where(low, a, b) + pltpu.roll(jnp.where(low, b, a), 4, 0)
        return jnp.where(low, a + pltpu.roll(a, 8 - shift, 0), b + pltpu.roll(b, shift, 0))

    def finish(i):
        for half in range(2):
            parts = [partial[(half * 8 + q) * 8 : (half * 8 + q + 1) * 8, :] for q in range(8)]
            for shift in (4, 2, 1):
                count = len(parts) // 2
                parts = [merge(parts[q], parts[q + count], shift) for q in range(count)]
            fsum[pl.ds(pl.multiple_of(i * 16 + half * 8, 8), 8), :] = parts[0]

    def step(g, i, carry):
        finish(jnp.maximum(i - 1, 0))
        w = [jnp.broadcast_to(pose[pl.ds(k * PLAIN + i, 1), :], (8, 128)) for k in range(3)]
        t = [jnp.broadcast_to(pose[pl.ds((3 + k) * PLAIN + i, 1), :], (8, 128)) for k in range(3)]
        w00, w11, w22 = w[0] * w[0], w[1] * w[1], w[2] * w[2]
        m00, m11, m22 = 1.0 + (w11 + w22), 1.0 + (w00 + w22), 1.0 + (w00 + w11)
        m01, m02, m12 = w[0] * w[1], w[0] * w[2], w[1] * w[2]
        total = [None] * 16
        for part in range(0, TILE, 16):
            seen = [seen_ref[k, i, part : part + 16, :].astype(jnp.float32) for k in range(3)]
            for h in range(2):
                at = part + h * 8
                x = [point[(g * 3 + k) * 64 + at : (g * 3 + k) * 64 + at + 8, :] for k in range(3)]
                o = [seen[k][h * 8 : (h + 1) * 8] for k in range(3)]
                r0 = (x[0] + t[0] - o[0]) + (w[1] * x[2] - w[2] * x[1])
                r1 = (x[1] + t[1] - o[1]) + (w[2] * x[0] - w[0] * x[2])
                r2 = (x[2] + t[2] - o[2]) + (w[0] * x[1] - w[1] * x[0])
                c = 1.0 / (scale + (r0 * r0 + r1 * r1 + r2 * r2))
                c0, c1, c2 = c * r0, c * r1, c * r2
                y = [c * x[k] for k in range(3)]
                terms = [
                    x[1] * c2 - x[2] * c1,
                    x[2] * c0 - x[0] * c2,
                    x[0] * c1 - x[1] * c0,
                    c0,
                    c1,
                    c2,
                    c,
                    y[0],
                    y[1],
                    y[2],
                    y[0] * x[0],
                    y[1] * x[1],
                    y[2] * x[2],
                    y[0] * x[1],
                    y[0] * x[2],
                    y[1] * x[2],
                ]
                total = terms if total[0] is None else [p + q for p, q in zip(total, terms)]
                terms = [
                    c * m00,
                    c * m11,
                    c * m22,
                    c * m01,
                    c * m02,
                    c * m12,
                    c0 - (w[1] * c2 - w[2] * c1),
                    c1 - (w[2] * c0 - w[0] * c2),
                    c2 - (w[0] * c1 - w[1] * c0),
                ]
                for q, term in enumerate(terms):
                    psum[g, q * 64 + at : q * 64 + at + 8, :] += term
        for q in range(16):
            partial[q * 8 : (q + 1) * 8, :] = total[q]
        return carry

    for g in range(GROUPS):
        lax.fori_loop(g * FOLDED, (g + 1) * FOLDED, functools.partial(step, g), 0)
    finish(PLAIN - 1)
    frame_sums = []
    for q in range(16):
        rows = fsum[pl.ds(q, PLAIN, stride=16), :]
        back = jnp.zeros((FOLDED, 128), jnp.float32)
        for g in range(GROUPS):
            mine = (lane >= g * EXTRA) & (lane < (g + 1) * EXTRA)
            back = jnp.where(mine, pltpu.roll(rows[g * FOLDED : (g + 1) * FOLDED], (g + 1) * EXTRA, 1), back)
        frame_sums += [rows, back]
    frame, position = names_ref[0:1, :], names_ref[1:2, :]
    held = position == row
    own = jnp.where(frame == lax.broadcasted_iota(jnp.int32, (16, 128), 0), scale, 0.0).astype(jnp.bfloat16)
    frames = sum(dot_t(own, piece) for piece in split(jnp.concatenate(frame_sums, axis=0), PARTS))
    for r in range(4):
        pair = frames[:, r * 128 : (r + 1) * 128]
        right[:, 2 * r, :] = half_turn(pair)
        right[:, 2 * r + 1, :] = pair
        sums[:, 10, r, :] = frames[:, (4 + r) * 128 : (5 + r) * 128]
    stores = [pltpu.make_async_copy(sums.at[:, 10], out_hbm.at[:, 10], sems.at[5])]
    stores[0].start()
    own = jnp.where(held, scale, 0.0).astype(jnp.bfloat16)
    for q in range(5):
        wide = 128 if q < 4 else 64
        part = unfold(psum[:, q * 128 : q * 128 + wide, :])
        part = sum(dot_t(own, piece) for piece in split(part, PARTS))
        if wide < 128:
            part = jnp.concatenate([part, jnp.zeros_like(part)], axis=1)
        part = part.reshape(16, 8, 128)
        if wide < 128:
            part = jnp.where(lax.broadcasted_iota(jnp.int32, part.shape, 2) < 64, part, right[...])
        sums[:, 2 * q] = part[:, 0:4]
        sums[:, 2 * q + 1] = part[:, 4:8]
        rows = slice(2 * q, 2 * q + 2)
        stores.append(pltpu.make_async_copy(sums.at[:, rows], out_hbm.at[:, rows], sems.at[q]))
        stores[-1].start()
    wait_all(stores)


def solve3(m00, m11, m22, m01, m02, m12, b0, b1, b2):
    i0 = 1.0 / m00
    l1, l2 = m01 * i0, m02 * i0
    d1 = m11 - l1 * m01
    e = m12 - l1 * m02
    i1 = 1.0 / d1
    l3 = e * i1
    d2 = m22 - l2 * m02 - l3 * e
    y1 = b1 - l1 * b0
    y2 = b2 - l2 * b0 - l3 * y1
    x2 = y2 / d2
    x1 = y1 * i1 - l3 * x2
    x0 = b0 * i0 - l1 * x1 - l2 * x2
    return x0, x1, x2


def new_poses(lower_sums, upper_sums, near_ref, link_ref, edge_ref, first_edge_ref, scratch):
    block, shard = own_frames(), lax.axis_index("tm")
    owners, shards = lax.axis_size("lm"), lax.axis_size("tm")
    lane = lanes((8, 128))
    current, before, after = (half_turn(near_ref[n, :, 128:256]) for n in range(3))
    outside = edge_ref[:, 0:128]
    initial, final = block == 0, block == owners - 1
    before = jnp.where(initial, outside, before)
    after = jnp.where(final, outside, after)
    previous = jnp.where(lane == 0, pltpu.roll(before, 65, 1), pltpu.roll(current, 1, 1))
    following = jnp.where(lane == 63, pltpu.roll(after, 63, 1), pltpu.roll(current, 127, 1))
    motion = link_ref[:, 0:128]
    motion_before = link_ref[:, 128:256]
    outside = pltpu.roll(first_edge_ref[:, 128:256], 65, 1)
    motion_before = jnp.where((lane == 0) & initial, outside, motion_before)
    ends = (lane[0:1] == 63) & final & (shard == shards - 1)
    starts = (lane[0:1] == 0) & initial & (shard == 0)
    weight_after = jnp.where(ends, 0.0, motion[6:7])
    weight_before = jnp.where(starts, 0.0, motion_before[6:7])
    scratch[0:8] = weight_before * (current - previous - motion_before) - weight_after * (
        following - current - motion
    )
    scratch[8:16] = half_turn(lower_sums)
    scratch[16:20] = upper_sums
    scratch[20:24] = half_turn(upper_sums)
    f = [scratch[8 + q : 9 + q, :] for q in range(8)]
    for r in range(4):
        f += [scratch[16 + r : 17 + r, :], scratch[20 + r : 21 + r, :]]
    g = [f[k] + scratch[k : k + 1, :] for k in range(6)]
    diagonal = weight_after + weight_before + damping
    s, c, m = f[6] + diagonal, f[7:10], f[10:16]
    inverse = 1.0 / s
    d = [c[k] * inverse for k in range(3)]
    n00 = m[1] + m[2] + diagonal - (c[1] * d[1] + c[2] * d[2])
    n11 = m[0] + m[2] + diagonal - (c[0] * d[0] + c[2] * d[2])
    n22 = m[0] + m[1] + diagonal - (c[0] * d[0] + c[1] * d[1])
    n01, n02, n12 = c[0] * d[1] - m[3], c[0] * d[2] - m[4], c[1] * d[2] - m[5]
    b0 = g[0] - (d[1] * g[5] - d[2] * g[4])
    b1 = g[1] - (d[2] * g[3] - d[0] * g[5])
    b2 = g[2] - (d[0] * g[4] - d[1] * g[3])
    x0, x1, x2 = solve3(n00, n11, n22, n01, n02, n12, b0, b1, b2)
    x3 = (g[3] + (c[1] * x2 - c[2] * x1)) * inverse
    x4 = (g[4] + (c[2] * x0 - c[0] * x2)) * inverse
    x5 = (g[5] + (c[0] * x1 - c[1] * x0)) * inverse
    for k, x in enumerate((x0, x1, x2, x3, x4, x5)):
        scratch[k : k + 1, :] = x
    return current - scratch[0:8]


def new_points(sums, near_ref):
    x = [near_ref[0, :, 0:128], half_turn(near_ref[0, :, 0:128]), near_ref[0, :, 128:256]]
    q = []
    for pair in sums:
        q += [pair, half_turn(pair)]
    moved = solve3(q[0] + damping, q[1] + damping, q[2] + damping, -q[3], -q[4], -q[5], q[6], q[7], q[8])
    return [x[k] - moved[k] for k in range(3)]


def total(sums_ref, part):
    parts = [sums_ref[d, part] for d in range(sums_ref.shape[0])]
    while len(parts) > 1:
        parts = [p + q for p, q in zip(parts[0::2], parts[1::2])]
    return parts[0]


def pair_total(sums_ref, k):
    return jnp.concatenate([total(sums_ref, 2 * k), total(sums_ref, 2 * k + 1)], axis=0)


def update_kernel(sums_ref, near_hbm, link_hbm, edge_hbm, copies_ref, sent_hbm, *scratch):
    near_ref, link_ref, edge_ref, sent, scratch, sems = scratch
    loads = load_all([near_hbm, link_hbm, edge_hbm], [near_ref, link_ref, edge_ref], sems)
    frames = pair_total(sums_ref, 4), total(sums_ref, 10)
    wait_all(loads)
    lower = lanes((8, 128)) < 64
    pose = new_poses(*frames, near_ref, link_ref, edge_ref, edge_ref, scratch)
    sent[...] = pose
    send = pltpu.make_async_copy(sent, sent_hbm, sems.at[3])
    send.start()
    x = new_points([pair_total(sums_ref, k) for k in range(4)] + [frames[0]], near_ref)
    left = jnp.where(lower, x[0], half_turn(x[1]))
    right = jnp.where(lower, x[2], half_turn(pose))
    for d in range(copies_ref.shape[0]):
        copies_ref[d, :, 0:128] = left
        copies_ref[d, :, 128:256] = right
    send.wait()


def last_poses_kernel(sums_ref, near_hbm, link_hbm, edge_hbm, first_edge_hbm, copies_ref, *scratch):
    near_ref, link_ref, edge_ref, first_edge_ref, scratch, sems = scratch
    sources = [near_hbm, link_hbm, edge_hbm, first_edge_hbm]
    loads = load_all(sources, [near_ref, link_ref, edge_ref, first_edge_ref], sems)
    frames = pair_total(sums_ref, 4), total(sums_ref, 10)
    wait_all(loads)
    pose = new_poses(*frames, near_ref, link_ref, edge_ref, first_edge_ref, scratch)
    lower = lanes((1, 128)) < 64
    for h in range(3):
        pair = jnp.where(lower, pose[2 * h : 2 * h + 1], half_turn(pose[2 * h + 1 : 2 * h + 2]))
        for d in range(copies_ref.shape[0]):
            copies_ref[d, :, h * 128 : (h + 1) * 128] = pair


def last_kernel(copies_ref, sums_ref, near_hbm, poses_ref, points_ref, near_ref, sem):
    load = pltpu.make_async_copy(near_hbm, near_ref, sem)
    load.start()
    owners = copies_ref.shape[0]
    for d in range(owners):
        block = (d + owners // 2 - 1) % owners
        for k in range(6):
            poses_ref[k : k + 1, block * 64 : (block + 1) * 64] = copies_ref[d, :, k * 64 : (k + 1) * 64]
    sums = [pair_total(sums_ref, k) for k in range(5)]
    load.wait()
    x = new_points(sums, near_ref)
    for k in range(3):
        for b in range(8):
            points_ref[k : k + 1, b * 64 : (b + 1) * 64] = x[k][b : b + 1, 0:64]


def call(kernel, outs, scratch, args, spaces, room=48):
    space = {"s": pltpu.SMEM, "v": pltpu.VMEM, "h": pltpu.HBM}
    specs = [pl.BlockSpec(memory_space=space[letter]) for letter in spaces]
    return pl.pallas_call(
        kernel,
        out_shape=outs,
        in_specs=specs[: len(args)],
        out_specs=specs[len(args) :],
        scratch_shapes=scratch,
        compiler_params=pltpu.CompilerParams(vmem_limit_bytes=67_043_328 - (room << 20)),
    )(*args)


def exchange(array):
    return lax.all_to_all(array, "lm", 0, 0, tiled=True)


def on_device(
    camera_poses,
    landmarks,
    odometry,
    odometry_info,
    observations,
    tile_frame,
    tile_block,
    tile_count,
    block_slot,
):
    owners, shards = lax.axis_size("lm"), lax.axis_size("tm")
    slots = observations.shape[0]
    f32 = jnp.float32
    seen = jnp.transpose(observations, (1, 2, 3, 0))
    to_edges = []
    for a in range(shards - 1):
        end, start = a * owners + owners // 2, (a + 1) * owners + owners // 2 + 1
        to_edges += [(end, start), (start, end)]

    def edges(array):
        return lax.ppermute(array, ("tm", "lm"), to_edges)

    def shape(*sizes):
        return jax.ShapeDtypeStruct(sizes, f32)

    def buffer(*sizes):
        return pltpu.VMEM(sizes, f32)

    dma = pltpu.SemaphoreType.DMA
    names = jax.ShapeDtypeStruct((8, 128), jnp.int32)
    copies, sent, link, *names = call(
        pack_kernel,
        [shape(owners, 8, 256), shape(8, 256), shape(8, 256), names, names],
        [
            buffer(*landmarks.shape),
            buffer(*camera_poses.shape),
            buffer(*odometry.shape),
            buffer(1, camera_poses.shape[1]),
            pltpu.VMEM((1, slots), jnp.int32),
            pltpu.VMEM((1, slots), jnp.int32),
            pltpu.VMEM(block_slot.shape, jnp.int32),
            buffer(8, 1024),
            buffer(8, 256),
            buffer(8, 256),
            buffer(8, 256),
            pltpu.VMEM((8, 128), jnp.int32),
            dma((11 + owners,)),
        ],
        [
            tile_count,
            landmarks,
            camera_poses,
            odometry,
            odometry_info[None, :],
            tile_frame[None, :],
            tile_block[None, :],
            block_slot,
        ],
        "shhhhhhhhhhhh",
        0,
    )
    (folded,) = call(
        fold_kernel,
        [jax.ShapeDtypeStruct((3, PLAIN, TILE, 128), seen.dtype)],
        [
            pltpu.VMEM(seen.shape, seen.dtype),
            dma((1 + GROUPS, 3)),
        ],
        [seen],
        "hv",
        14,
    )
    first_edge = None
    for iteration in range(ITERS):
        window = exchange(copies)
        edge = edges(sent)
        sums, near = call(
            tiles_kernel,
            [shape(owners, 11, 4, 128), shape(3, 8, 256)],
            [
                buffer(3, 8, 256),
                buffer(6 * PLAIN, 128),
                dma,
                buffer(GROUPS * 192, 128),
                buffer(16 * PLAIN, 128),
                buffer(GROUPS, 576, 128),
                buffer(128, 128),
                buffer(owners, 8, 128),
                buffer(owners, 11, 4, 128),
                dma((6,)),
            ],
            [window, names[iteration], folded],
            "vvvhh",
            14,
        )
        sums = exchange(sums)
        if iteration == 0:
            first_edge = edge
            copies, sent = call(
                update_kernel,
                [shape(owners, 8, 256), shape(8, 128)],
                [buffer(3, 8, 256), buffer(8, 256), buffer(8, 256), buffer(8, 128), buffer(24, 128), dma((4,))],
                [sums, near, link, edge],
                "vhhhvh",
            )
    (copies,) = call(
        last_poses_kernel,
        [shape(owners, 1, 384)],
        [buffer(3, 8, 256), buffer(8, 256), buffer(8, 128), buffer(8, 256), buffer(24, 128), dma((4,))],
        [sums, near, link, edge, first_edge],
        "vhhhhv",
    )
    poses, points = call(
        last_kernel,
        [shape(*camera_poses.shape), shape(*landmarks.shape)],
        [buffer(3, 8, 256), dma],
        [exchange(copies), sums, near],
        "vvhvv",
    )
    return (poses, points)


def solution(mesh):
    return jax.shard_map(
        on_device,
        mesh=mesh,
        in_specs=(
            P(None, "tm"),
            P(None, ("tm", "lm")),
            P(None, "tm"),
            P("tm"),
            P(("tm", "lm"), None, None, None),
            P(("tm", "lm")),
            P(("tm", "lm")),
            P(("tm", "lm")),
            P("tm", None),
        ),
        out_specs=(P(None, "tm"), P(None, ("tm", "lm"))),
        check_vma=False,
    )
```
